128 devices in a mesh: section: 4 (over x), expert: 32 (over y, z, core).
Axes of the slice: x: 4, y: 4, z: 4, core: 2. Of those that a mesh axis runs over, the one named last changes fastest.
Arguments:
- section_inputs: bfloat16 [4, 3, 2048, 2048], P('section', None, 'expert'), may hold values from -6 to 6
- cotangent: bfloat16 [3, 2048, 2048], P(None, 'expert'), may hold values from -6 to 6
- expert_ids: int32 [4, 3, 2048, 2], P('section', None, 'expert'), may hold values from 0 to 31, all different within a row; in each aligned block of 64 rows (0 to 63, 64 to 127, ..., all dimensions but the last counted through in order) at most 6 rows name the same one
- route_weights: float32 [4, 3, 2048, 2], P('section', None, 'expert'), may hold values from 0.2 to 1
- w_gate: bfloat16 [4, 32, 2048, 512], P('section', 'expert'), may hold values from -0.125 to 0.125
- w_up: bfloat16 [4, 32, 2048, 512], P('section', 'expert'), may hold values from -0.125 to 0.125
- w_down: bfloat16 [4, 32, 512, 2048], P('section', 'expert'), may hold values from -0.25 to 0.25
Outputs:
- input_grads: bfloat16 [4, 3, 2048, 2048], P('section', None, 'expert')
- grad_gate: float32 [4, 32, 2048, 512], P('section', 'expert')
- grad_up: float32 [4, 32, 2048, 512], P('section', 'expert')
- precond_down: float32 [4, 32, 512, 2048], P('section', 'expert')
The draws below stay inside these ranges and needn't reach their ends.
Inputs may be any that keep to these rules, and one draw needn't show every extreme that they name: `expert_ids`: each token names two different experts. In each aligned block of 64 rows (the rows of one device in one layer and micro-batch) no expert is named by more than 6 rows, a bound that some block reaches.
All inputs are finite; a program needn't handle non-finite values.
Results may differ from the reference program's by a relative error of at most 0.013.
Values may be sent and summed in bfloat16 or wider, within the bound.
No kernel may reach another device: no remote copies, remote signals or barrier semaphores. Data moves between devices by JAX's collectives and lax.ppermute only.
A program may use at most 192 MiB of HBM per device.

```python
import math
import jax
import jax.numpy as jnp
import numpy as np
from jax import lax

D = 2048
FF_E = 512
ROWS_DEV = 64
TICKS = 3
NS_ITERS = 5
LAYERS = 4
EXPERTS = 32
TOKENS = 2048
CAP = 6
N_EXPERT = 32


def block_levels(key, extent, pieces, smallest, largest):
    def one(axis_at, parts):
        steps = jax.random.uniform(jax.random.fold_in(jax.random.fold_in(key, 6), axis_at), (parts,), jnp.float32, smallest / len(pieces), largest / len(pieces))
        return jnp.repeat(jnp.exp(steps), extent[axis_at] // parts).reshape((-1,) + (1,) * (len(extent) - axis_at - 1))

    loudness = one(*pieces[0])
    for cut in pieces[1:]:
        loudness = loudness * one(*cut)
    return loudness


def assign_block(stream_key, own, number, rows, number_of, top, reach, lean):
    order = jax.random.permutation(stream_key, number_of)
    crowded, ordinary = portions_of(number_of, rows * top, reach, lean, True), portions_of(number_of, rows * top, reach, lean, False)
    places = jnp.arange(number_of)

    def named(tallies, turn):
        used = int((tallies > 0).sum())
        fixed = max(1, used // 4)
        shifted = fixed + (places - fixed + turn * (used - fixed)) % max(1, number_of - fixed)
        return jnp.zeros((number_of,), jnp.int32).at[order[jnp.where(places < fixed, places, shifted)]].set(jnp.asarray(tallies, jnp.int32))

    tallies = jnp.where(number % 4 == 0, named(crowded, number // 4), named(ordinary, number - number // 4 - 1))
    mixed = jax.random.permutation(jax.random.fold_in(own, 3), number_of)
    donor, receiver = mixed[0:number_of // 2 * 2:2], mixed[1:number_of // 2 * 2:2]
    margin = jnp.minimum(tallies[donor] - 1, reach - tallies[receiver]) // 2
    margin = jnp.where((donor == order[0]) | (receiver == order[0]) | (tallies[receiver] == 0), 0, jnp.maximum(margin, 0))
    shifted = jax.random.randint(jax.random.fold_in(own, 4), (number_of // 2,), 0, 1 << 20) % (margin + 1)
    tallies = tallies.at[donor].add(-shifted).at[receiver].add(shifted)
    members = jnp.searchsorted(jnp.cumsum(tallies), jnp.arange(rows * top), side="right").astype(jnp.int32)
    grid = members.reshape(top, rows).T
    grid = grid[jax.random.permutation(jax.random.fold_in(own, 1), rows)]
    turn = jax.random.randint(jax.random.fold_in(own, 2), (rows, 1), 0, top)
    return jnp.take_along_axis(grid, (jnp.arange(top)[None, :] + turn) % top, axis=1)


def portions_of(count, total, bound, lean, full):
    loads = [(1 << 20) // math.isqrt(grade ** lean) + 1 for grade in range(1, count + 1)]
    largest = bound if full else min(bound, max(-(-total // count), total * loads[0] // sum(loads)))
    least = 1 if total - largest >= count - 1 else 0
    given, spare = [largest] + [least] * (count - 1), total - largest - least * (count - 1)
    while spare > 0:
        free = [i for i in range(1, count) if given[i] < largest] or [i for i in range(1, count) if given[i] < bound]
        mass, left = sum([loads[i] for i in free]), spare
        for i in free:
            addition = min(bound - given[i], max(1, left * loads[i] // mass), spare)
            given[i] = given[i] + addition
            spare = spare - addition
    return np.array(given)


def gaussian(rng, dims, spread, limit, split=(), kind=jnp.bfloat16):
    gain = block_levels(rng, dims, split, -0.22, 0.18) if split else 1.0
    values = jax.random.normal(rng, dims, jnp.float32) * spread * gain
    return jnp.minimum(jnp.maximum(values, -limit), limit).astype(kind)


def setup_inputs(seed: int = 0) -> dict:
    key_list = jax.random.split(jax.random.key(seed), 8)
    section_inputs = gaussian(key_list[0], (LAYERS, TICKS, TOKENS, D), 1.0, 6.0, ((0, 4), (2, 32)))
    cotangent = gaussian(key_list[1], (TICKS, TOKENS, D), 1.0, 6.0, ((1, 32),))
    expert_ids_keys = jax.random.split(jax.random.fold_in(key_list[2], 1), LAYERS * TICKS * TOKENS // ROWS_DEV)
    expert_ids_turns = jax.random.permutation(jax.random.fold_in(key_list[2], 3), LAYERS * TICKS * TOKENS // ROWS_DEV)
    expert_ids = jax.vmap(lambda own, number: assign_block(jax.random.fold_in(key_list[2], 2), own, number, ROWS_DEV, EXPERTS, 2, CAP, 2))(expert_ids_keys, expert_ids_turns).reshape((LAYERS, TICKS, TOKENS, 2))
    route_weights = jnp.clip(0.2 + 0.8 * jax.random.uniform(key_list[3], (LAYERS, TICKS, TOKENS, 2), jnp.float32) ** block_levels(key_list[3], (LAYERS, TICKS, TOKENS, 2), ((0, 4), (2, 32)), -0.2, 0.2), 0.2, 1.0)
    w_gate = gaussian(key_list[4], (LAYERS, EXPERTS, D, FF_E), D ** -0.5, 0.125, ((0, 4), (1, 32)))
    w_up = gaussian(key_list[5], (LAYERS, EXPERTS, D, FF_E), D ** -0.5, 0.125, ((0, 4), (1, 32)))
    w_down = gaussian(key_list[6], (LAYERS, EXPERTS, FF_E, D), FF_E ** -0.5, 0.25, ((0, 4), (1, 32)))
    return dict(section_inputs=section_inputs, cotangent=cotangent, expert_ids=expert_ids, route_weights=route_weights, w_gate=w_gate, w_up=w_up, w_down=w_down)


damping = 0.1
epsilon = 1e-06

def silu_slope(values):
    logistic = jax.nn.sigmoid(values)
    return logistic * (1.0 + values * (1.0 - logistic))

def inverse_root(curvature, iterations):
    identity_m = jnp.eye(curvature.shape[0], dtype=jnp.float32)
    frobenius = jnp.sqrt(jnp.sum(curvature * curvature))
    current = curvature / frobenius
    result = identity_m * frobenius ** (-0.25)
    for turn_index in range(iterations):
        factor = (5.0 * identity_m - current) * 0.25
        result = jnp.dot(result, factor, precision=lax.Precision.HIGHEST)
        square = jnp.dot(factor, factor, precision=lax.Precision.HIGHEST)
        fourth = jnp.dot(square, square, precision=lax.Precision.HIGHEST)
        current = jnp.dot(fourth, current, precision=lax.Precision.HIGHEST)
    return result

def reference(section_inputs, cotangent, expert_ids, route_weights, w_gate, w_up, w_down):
    f32 = jnp.float32
    bf16 = jnp.bfloat16
    slots_all = N_EXPERT * CAP
    cots = [cotangent[tick_index] for tick_index in range(TICKS)]
    grads_in = [[None] * TICKS for layer_index in range(LAYERS)]
    gate_list = [None] * LAYERS
    up_list = [None] * LAYERS
    pre_list = [None] * LAYERS
    for layer in reversed(range(LAYERS)):
        weight_gate = w_gate[layer].astype(f32)
        weight_up = w_up[layer].astype(f32)
        weight_down = w_down[layer].astype(f32)
        acc_gate = jnp.zeros((EXPERTS, D, FF_E), f32)
        acc_up = jnp.zeros((EXPERTS, D, FF_E), f32)
        acc_down = jnp.zeros((EXPERTS, FF_E, D), f32)
        acc_gram = jnp.zeros((EXPERTS, FF_E, FF_E), f32)
        for tick in range(TICKS):
            current_cot = cots[tick]
            flat_ids = expert_ids[layer, tick].reshape(N_EXPERT, ROWS_DEV * 2)
            onehot = (flat_ids[:, :, None] == jnp.arange(EXPERTS, dtype=jnp.int32)[None, None, :]).astype(jnp.int32)
            ranking = lax.optimization_barrier(jnp.sum((jnp.cumsum(onehot, axis=1) - onehot) * onehot, axis=2))
            slot = (jnp.arange(N_EXPERT, dtype=jnp.int32)[:, None] * CAP + ranking).astype(jnp.int32)
            rows_x = jnp.repeat(section_inputs[layer, tick], 2, axis=0).reshape(N_EXPERT, ROWS_DEV * 2, D)
            scaled = (route_weights[layer, tick][:, :, None] * current_cot.astype(f32)[:, None, :]).astype(bf16)
            scaled = scaled.reshape(N_EXPERT, ROWS_DEV * 2, D)
            buf_x = jnp.zeros((EXPERTS, slots_all, D), bf16).at[flat_ids, slot].set(rows_x)
            buf_g = jnp.zeros((EXPERTS, slots_all, D), bf16).at[flat_ids, slot].set(scaled)
            xs32 = buf_x.astype(f32)
            gs32 = buf_g.astype(f32)
            gate = jnp.einsum('esd,edf->esf', xs32, weight_gate)
            up_proj = jnp.einsum('esd,edf->esf', xs32, weight_up)
            soft_gate = jax.nn.silu(gate)
            hidden = (soft_gate * up_proj).astype(bf16)
            grad_hidden = jnp.einsum('esd,efd->esf', gs32, weight_down)
            d_gate = (grad_hidden * up_proj * silu_slope(gate)).astype(bf16)
            d_up = (grad_hidden * soft_gate).astype(bf16)
            dg32 = d_gate.astype(f32)
            du32 = d_up.astype(f32)
            hid32 = hidden.astype(f32)
            expert_back = (jnp.einsum('esf,edf->esd', dg32, weight_gate) + jnp.einsum('esf,edf->esd', du32, weight_up)).astype(bf16)
            acc_gate = acc_gate + jnp.einsum('esd,esf->edf', xs32, dg32)
            acc_up = acc_up + jnp.einsum('esd,esf->edf', xs32, du32)
            acc_down = acc_down + jnp.einsum('esf,esd->efd', hid32, gs32)
            acc_gram = acc_gram + jnp.einsum('esf,esg->efg', hid32, hid32)
            back = expert_back[flat_ids, slot].astype(f32).reshape(TOKENS, 2, D).sum(axis=1)
            new_cot = (current_cot.astype(f32) + back).astype(bf16)
            grads_in[layer][tick] = new_cot
            cots[tick] = new_cot
        traces = jnp.trace(acc_gram, axis1=1, axis2=2)[:, None, None]
        curvature = acc_gram * (FF_E / (traces + epsilon)) + damping * jnp.eye(FF_E, dtype=f32)[None]
        roots = jax.vmap(lambda matrix: inverse_root(matrix, NS_ITERS))(curvature)
        pre_list[layer] = jnp.matmul(roots, acc_down, precision=lax.Precision.HIGHEST)
        gate_list[layer] = acc_gate
        up_list[layer] = acc_up
    input_grads = jnp.stack([jnp.stack(grads_in[layer_index]) for layer_index in range(LAYERS)])
    return (input_grads, jnp.stack(gate_list), jnp.stack(up_list), jnp.stack(pre_list))
```

```python
import functools

import jax
import jax.numpy as jnp
from jax import lax
from jax.experimental import pallas as pl
from jax.experimental.pallas import tpu as pltpu
from jax.sharding import PartitionSpec as P

NS_ITERS = 5

damping = 0.1
epsilon = 1e-06

LANES = 128
F32 = jnp.float32
BF16 = jnp.bfloat16
VM = pltpu.VMEM
SM = pltpu.SMEM
PARAMS = pltpu.CompilerParams(vmem_limit_bytes=60 << 20)
LIMITS = {"dispatch": 55000000, "backward": 55000000, "combine": 54000000, "first": 53500000, "forward": 62000000}


def estimate(flops, moved):
    return pl.CostEstimate(flops=int(flops), bytes_accessed=int(moved), transcendentals=0)


def dot(a, b, ad, bd):
    return lax.dot_general(a, b, (((ad,), (bd,)), ((), ())), preferred_element_type=F32)


HBM = pltpu.HBM
ANY = pl.ANY


def fold_rows(flat_ref, cur_ref, rows, fold):
    for part in range(fold):
        cur_ref[pl.ds(part, rows, stride=fold), :] = flat_ref[
            :, part * LANES : (part + 1) * LANES
        ].astype(F32)


def load_current(info_ref, top_ref, inc_ref, flat_ref, buf_ref, cur_ref, sem, rows, fold):
    def from_top():
        copy = pltpu.make_async_copy(top_ref.at[info_ref[0]], flat_ref, sem)
        copy.start()
        copy.wait()
        fold_rows(flat_ref, cur_ref, rows, fold)

    def from_above():
        copy = pltpu.make_async_copy(inc_ref, buf_ref, sem)
        copy.start()
        copy.wait()
        cur_ref[...] = buf_ref[...].astype(F32)

    if inc_ref is None:
        from_top()
    elif top_ref is None:
        from_above()
    else:
        pl.when(info_ref[1] == 1)(from_top)
        pl.when(info_ref[1] == 0)(from_above)


def place_rows(
    src_ref, scale_ref, plain, base, first, count, fold, group, stride, offset, cur_ref, out_ref
):
    def some(step, carry):
        for part in range(group):
            place = step * group + part
            row = src_ref[base + place]
            factor = scale_ref[base + place]
            if plain:
                factor = jnp.where(factor > 0.0, 1.0, 0.0)
            tile = cur_ref[pl.ds(pl.multiple_of(row * fold, fold), fold), :]
            out_ref[pl.ds(pl.multiple_of((step * stride + offset + part) * fold, fold), fold), :] = (
                tile * factor
            ).astype(BF16)
        return carry

    lax.fori_loop(first // group, (first + count) // group, some, 0)


CHUNKS = 4


def dispatch_kernel(
    has_top, has_inc, plain, rows, slots, fold, group, info_ref, src_ref, scale_ref, *refs
):
    refs = list(refs)
    top_ref = refs.pop(0) if has_top else None
    inc_ref = refs.pop(0) if has_inc else None
    out_ref, flat_ref, buf_ref, cur_ref, put_ref, sems = refs
    load_current(info_ref, top_ref, inc_ref, flat_ref, buf_ref, cur_ref, sems.at[0], rows, fold)
    base = info_ref[0] * slots
    count = slots // CHUNKS
    copies = []
    for chunk in range(CHUNKS):
        place_rows(
            src_ref, scale_ref, plain, base, chunk * count, count, fold, group, group, 0,
            cur_ref, put_ref,
        )
        part = pl.ds(chunk * count * fold, count * fold)
        copies.append(
            pltpu.make_async_copy(put_ref.at[part], out_ref.at[part], sems.at[1 + chunk])
        )
        copies[-1].start()
    for copy in copies:
        copy.wait()


def dispatch(info, src, scale, top, inc, plain, rows, slots, fold, group):
    arrays = [value for value in (top, inc) if value is not None]
    return pl.pallas_call(
        functools.partial(
            dispatch_kernel, top is not None, inc is not None, plain, rows, slots, fold, group
        ),
        out_shape=jax.ShapeDtypeStruct((slots * fold, LANES), BF16),
        grid_spec=pltpu.PrefetchScalarGridSpec(
            num_scalar_prefetch=2,
            grid=(1,),
            in_specs=[pl.BlockSpec(memory_space=SM)]
            + [pl.BlockSpec(memory_space=HBM)] * (top is not None)
            + [pl.BlockSpec(memory_space=ANY)] * (inc is not None),
            out_specs=pl.BlockSpec(memory_space=HBM),
            scratch_shapes=[
                VM((rows, fold * LANES), BF16),
                VM((rows * fold, LANES), BF16),
                VM((rows * fold, LANES), F32),
                VM((slots * fold, LANES), BF16),
                pltpu.SemaphoreType.DMA((1 + CHUNKS,)),
            ],
        ),
        compiler_params=pltpu.CompilerParams(vmem_limit_bytes=LIMITS["dispatch"]),
        cost_estimate=estimate(1e6, 4e6),
        name="dispatch",
    )(info, src, scale, *arrays)


def first_kernel(rows, slots, fold, group, src_ref, scale_ref, x_ref, top_ref, out_ref, *rest):
    buf_x, buf_g, cur_x, cur_g, put_ref, sems = rest
    copies = [
        pltpu.make_async_copy(x_ref.at[0], buf_x, sems.at[0]),
        pltpu.make_async_copy(top_ref.at[0], buf_g, sems.at[1]),
    ]
    for copy in copies:
        copy.start()
    copies[0].wait()
    fold_rows(buf_x, cur_x, rows, fold)
    copies[1].wait()
    fold_rows(buf_g, cur_g, rows, fold)
    count = slots // CHUNKS
    copies = []
    for chunk in range(CHUNKS):
        for offset, plain, cur in ((0, True, cur_x), (group, False, cur_g)):
            place_rows(
                src_ref, scale_ref, plain, 0, chunk * count, count, fold, group, 2 * group, offset,
                cur, put_ref,
            )
        part = pl.ds(chunk * count * fold * 2, count * fold * 2)
        copies.append(
            pltpu.make_async_copy(put_ref.at[part], out_ref.at[part], sems.at[2 + chunk])
        )
        copies[-1].start()
    for copy in copies:
        copy.wait()


def first_dispatch(src, scale, x, top, rows, slots, fold, group):
    return pl.pallas_call(
        functools.partial(first_kernel, rows, slots, fold, group),
        out_shape=jax.ShapeDtypeStruct((2 * slots * fold, LANES), BF16),
        in_specs=[pl.BlockSpec(memory_space=SM)] * 2 + [pl.BlockSpec(memory_space=HBM)] * 2,
        out_specs=pl.BlockSpec(memory_space=HBM),
        scratch_shapes=[VM((rows, fold * LANES), BF16)] * 2
        + [VM((rows * fold, LANES), F32)] * 2
        + [VM((2 * slots * fold, LANES), BF16), pltpu.SemaphoreType.DMA((2 + CHUNKS,))],
        compiler_params=PARAMS,
        cost_estimate=estimate(1e6, 4e6),
        name="first_dispatch",
    )(src, scale, x, top)


def combine_kernel(has_top, has_inc, last, rows, fold, info_ref, slot_ref, *refs):
    refs = list(refs)
    top_ref = refs.pop(0) if has_top else None
    inc_ref = refs.pop(0) if has_inc else None
    came_hbm = refs.pop(0)
    if last:
        old_ref, flat_ref, top_buf, buf_ref, cur_ref, came_ref, sems = refs
    else:
        new_ref, top_buf, buf_ref, cur_ref, came_ref, sems = refs
    came_copy = pltpu.make_async_copy(came_hbm, came_ref, sems.at[1])
    came_copy.start()
    load_current(info_ref, top_ref, inc_ref, top_buf, buf_ref, cur_ref, sems.at[0], rows, fold)
    came_copy.wait()
    base = info_ref[0] * rows * 2

    def some(step, carry):
        for part in range(4):
            row = step * 4 + part
            first = slot_ref[base + 2 * row]
            second = slot_ref[base + 2 * row + 1]
            here = pl.ds(pl.multiple_of(row * fold, fold), fold)
            one = came_ref[pl.ds(pl.multiple_of(first * fold, fold), fold), :].astype(F32)
            two = came_ref[pl.ds(pl.multiple_of(second * fold, fold), fold), :].astype(F32)
            total = cur_ref[here, :] + (one + two)
            if last:
                cur_ref[here, :] = total
            else:
                buf_ref[here, :] = total.astype(BF16)
        return carry

    if not last:
        half = rows // 2
        copies = []
        for chunk in range(2):
            lax.fori_loop(chunk * half // 4, (chunk + 1) * half // 4, some, 0)
            part = pl.ds(chunk * half * fold, half * fold)
            copies.append(
                pltpu.make_async_copy(buf_ref.at[part], new_ref.at[part], sems.at[2 + chunk])
            )
            copies[-1].start()
        for copy in copies:
            copy.wait()
    else:
        lax.fori_loop(0, rows // 4, some, 0)
        unfold_rows(info_ref, cur_ref, old_ref, flat_ref, rows, fold)


def unfold_rows(info_ref, cur_ref, old_ref, flat_ref, rows, fold):
    @pl.when(info_ref[2] == 1)
    def _():
        for part in range(fold):
            flat_ref[0, :, part * LANES : (part + 1) * LANES] = cur_ref[
                pl.ds(part, rows, stride=fold), :
            ].astype(BF16)

    @pl.when(info_ref[2] == 0)
    def _():
        flat_ref[...] = old_ref[...]


def combine(info, slot, top, inc, came, rows, slots, fold, results=None):
    last = results is not None
    arrays = [value for value in (top, inc, came) if value is not None]
    specs = [pl.BlockSpec(memory_space=HBM)] * (top is not None)
    specs += [pl.BlockSpec(memory_space=ANY)] * (len(arrays) - len(specs))
    aliases = {}
    out_shape = jax.ShapeDtypeStruct((rows * fold, LANES), BF16)
    out_specs = pl.BlockSpec(memory_space=HBM)
    if last:
        block = pl.BlockSpec((1, rows, fold * LANES), lambda i, info, *_: (info[0], 0, 0))
        aliases = {2 + len(arrays): 0}
        out_shape = jax.ShapeDtypeStruct(results.shape, BF16)
        arrays, specs, out_specs = arrays + [results], specs + [block], block
    return pl.pallas_call(
        functools.partial(combine_kernel, top is not None, inc is not None, last, rows, fold),
        out_shape=out_shape,
        grid_spec=pltpu.PrefetchScalarGridSpec(
            num_scalar_prefetch=2,
            grid=(1,),
            in_specs=specs,
            out_specs=out_specs,
            scratch_shapes=[
                VM((rows, fold * LANES), BF16),
                VM((rows * fold, LANES), BF16),
                VM((rows * fold, LANES), F32),
                VM((slots * fold, LANES), BF16),
                pltpu.SemaphoreType.DMA((4,)),
            ],
        ),
        input_output_aliases=aliases,
        compiler_params=pltpu.CompilerParams(vmem_limit_bytes=LIMITS["combine"]),
        cost_estimate=estimate(1e6, 4e6),
        name="combine",
    )(info, slot, *arrays)


def keep_kernel(rows, fold, aliased, info_ref, new_ref, *refs):
    old_ref, flat_ref, cur_ref = refs if aliased else (None, *refs)
    cur_ref[...] = new_ref[...].astype(F32)
    if aliased:
        unfold_rows(info_ref, cur_ref, old_ref, flat_ref, rows, fold)
    else:
        for part in range(fold):
            flat_ref[0, :, part * LANES : (part + 1) * LANES] = cur_ref[
                pl.ds(part, rows, stride=fold), :
            ].astype(BF16)


def keep_rows(info, new, results, ticks, rows, fold):
    block = pl.BlockSpec((1, rows, fold * LANES), lambda i, info: (info[0], 0, 0))
    more = [] if results is None else [results]
    return pl.pallas_call(
        functools.partial(keep_kernel, rows, fold, results is not None),
        out_shape=jax.ShapeDtypeStruct((ticks, rows, fold * LANES), BF16),
        grid_spec=pltpu.PrefetchScalarGridSpec(
            num_scalar_prefetch=1,
            grid=(1,),
            in_specs=[pl.BlockSpec((rows * fold, LANES), lambda i, info: (0, 0))] + [block] * len(more),
            out_specs=block,
            scratch_shapes=[VM((rows * fold, LANES), F32)],
        ),
        input_output_aliases={2: 0} if more else {},
        compiler_params=PARAMS,
        cost_estimate=estimate(1e6, 1e6),
        name="keep_rows",
    )(info, new, *more)


def gradients_kernel(lead_ref, dg_ref, du_ref, xs_ref, gs_ref, gate_ref, up_ref, down_ref):
    rows_x = xs_ref[...]
    gate_ref[...] = dot(rows_x, dg_ref[...], 0, 0)
    up_ref[...] = dot(rows_x, du_ref[...], 0, 0)
    down_ref[...] = dot(lead_ref[...], gs_ref[...], 1, 0)


def gradients(lead, dg, du, xs, gs):
    depth, width = xs.shape
    hidden = dg.shape[1]
    wide = 256

    def whole(value):
        return pl.BlockSpec(value.shape, lambda i: (0, 0))

    columns = pl.BlockSpec((depth, wide), lambda i: (0, i))
    rows_out = pl.BlockSpec((wide, hidden), lambda i: (i, 0))
    return pl.pallas_call(
        gradients_kernel,
        out_shape=(
            jax.ShapeDtypeStruct((width, hidden), F32),
            jax.ShapeDtypeStruct((width, hidden), F32),
            jax.ShapeDtypeStruct((hidden, width), F32),
        ),
        grid=(width // wide,),
        in_specs=[whole(lead), whole(dg), whole(du), columns, columns],
        out_specs=(rows_out, rows_out, pl.BlockSpec((hidden, wide), lambda i: (0, i))),
        compiler_params=PARAMS,
        cost_estimate=estimate(6 * hidden * width * depth, 18e6),
        name="gradients",
    )(lead, dg, du, xs, gs)


def forward_kernel(aliased, tick, slots, fold, experts, got_hbm, wg_hbm, wu_hbm, *refs):
    refs = list(refs)
    if aliased:
        refs.pop(0)
    xs_hbm, hid_hbm, fac_hbm, got, wg, wu, scr, xs, hid, fac, sems = refs
    copies = [
        pltpu.make_async_copy(got_hbm.at[:, pl.ds(0, got.shape[1])], got, sems.at[0]),
        pltpu.make_async_copy(wg_hbm, wg, sems.at[1]),
        pltpu.make_async_copy(wu_hbm, wu, sems.at[2]),
    ]
    for copy in copies:
        copy.start()
    copies[0].wait()
    scr[...] = got[...].astype(F32).reshape(slots * fold, LANES)
    for part in range(fold):
        xs[:, part * LANES : (part + 1) * LANES] = scr[pl.ds(part, slots, stride=fold), :].astype(
            BF16
        )
    puts = [
        pltpu.make_async_copy(xs, xs_hbm.at[pl.ds(tick * slots, slots)], sems.at[3]),
        pltpu.make_async_copy(hid, hid_hbm, sems.at[4]),
        pltpu.make_async_copy(fac, fac_hbm, sems.at[5]),
    ]
    puts[0].start()
    rows_x = xs[...]
    copies[1].wait()
    gate = dot(rows_x, wg[...], 1, 0)
    copies[2].wait()
    up = dot(rows_x, wu[...], 1, 0)
    logistic = jax.nn.sigmoid(gate)
    soft = gate * logistic
    fac[0] = up * (logistic * (1.0 + gate * (1.0 - logistic)))
    fac[1] = soft
    puts[2].start()
    hid[...] = (soft * up).astype(BF16)
    puts[1].start()
    for put in puts:
        put.wait()


def forward(got, wg, wu, xs_all, tick, ticks, slots, fold, limit):
    experts = got.shape[0]
    width, hidden = wg.shape
    arrays = [got, wg, wu]
    aliases = {}
    if xs_all is not None:
        arrays.append(xs_all)
        aliases = {3: 0}
    hbm_spec = pl.BlockSpec(memory_space=HBM)
    return pl.pallas_call(
        functools.partial(forward_kernel, xs_all is not None, tick, slots, fold, experts),
        out_shape=(
            jax.ShapeDtypeStruct((ticks * slots, width), BF16),
            jax.ShapeDtypeStruct((slots, hidden), BF16),
            jax.ShapeDtypeStruct((2, slots, hidden), F32),
        ),
        in_specs=[pl.BlockSpec(memory_space=ANY)] + [hbm_spec] * (len(arrays) - 1),
        out_specs=(hbm_spec,) * 3,
        scratch_shapes=[
            VM((experts, slots * fold // experts, LANES), BF16),
            VM((width, hidden), BF16),
            VM((width, hidden), BF16),
            VM((slots * fold, LANES), F32),
            VM((slots, width), BF16),
            VM((slots, hidden), BF16),
            VM((2, slots, hidden), F32),
            pltpu.SemaphoreType.DMA((6,)),
        ],
        input_output_aliases=aliases,
        compiler_params=pltpu.CompilerParams(vmem_limit_bytes=limit),
        cost_estimate=estimate(4 * slots * width * hidden, 8e6),
        name="forward",
    )(*arrays)


def backward_kernel(
    aliased, count, slots, fold, info_ref, got_hbm, wd_hbm, wg_hbm, wu_hbm, *refs
):
    refs = list(refs)
    fac_hbm = refs[:count]
    del refs[:count]
    if aliased:
        del refs[:3]
    out_hbm, gs_hbm, dg_hbm, du_hbm, got, wd, wg, wu, fac, scr, gs, dg, du, out, sems = refs
    begin = got_hbm.shape[1] - got.shape[1]
    copies = [
        pltpu.make_async_copy(got_hbm.at[:, pl.ds(begin, got.shape[1])], got, sems.at[0]),
        pltpu.make_async_copy(wd_hbm, wd, sems.at[1]),
        pltpu.make_async_copy(wg_hbm, wg, sems.at[2]),
        pltpu.make_async_copy(wu_hbm, wu, sems.at[3]),
    ]
    copies[0].start()
    copies[1].start()
    for which in range(count):

        @pl.when(info_ref[0] == which)
        def _(which=which):
            pltpu.make_async_copy(fac_hbm[which], fac, sems.at[4]).start()

    copies[2].start()
    copies[3].start()
    copies[0].wait()
    scr[...] = got[...].astype(F32).reshape(slots * fold, LANES)
    for part in range(fold):
        gs[:, part * LANES : (part + 1) * LANES] = scr[pl.ds(part, slots, stride=fold), :].astype(
            BF16
        )
    mine = pl.ds(pl.multiple_of(info_ref[0] * slots, slots), slots)
    keeps = [
        pltpu.make_async_copy(gs, gs_hbm.at[mine], sems.at[5]),
        pltpu.make_async_copy(dg, dg_hbm.at[mine], sems.at[6]),
        pltpu.make_async_copy(du, du_hbm.at[mine], sems.at[7]),
    ]
    copies[1].wait()
    grad_hidden = dot(gs[...], wd[...], 1, 1)
    pltpu.make_async_copy(fac_hbm[0], fac, sems.at[4]).wait()
    d_gate = (grad_hidden * fac[0]).astype(BF16)
    d_up = (grad_hidden * fac[1]).astype(BF16)
    dg[...] = d_gate
    du[...] = d_up
    copies[2].wait()
    copies[3].wait()

    @pl.when(info_ref[2] == 1)
    def _():
        for keep in keeps:
            keep.start()

    puts = []
    wide = 4
    for part in range(0, fold, wide):
        cols = slice(part * LANES, (part + wide) * LANES)
        back = dot(d_gate, wg[cols, :], 1, 1) + dot(d_up, wu[cols, :], 1, 1)
        for inner in range(wide):
            scr[pl.ds(part + inner, slots, stride=fold), :] = back[
                :, inner * LANES : (inner + 1) * LANES
            ]
    size = slots * fold // 2
    for chunk in range(2):
        some = pl.ds(chunk * size, size)
        out[some, :] = scr[some, :].astype(BF16)
        puts.append(pltpu.make_async_copy(out.at[some], out_hbm.at[some], sems.at[8 + chunk]))
        puts[-1].start()
    for put in puts:
        put.wait()

    @pl.when(info_ref[2] == 1)
    def _():
        for keep in keeps:
            keep.wait()


def backward(info, got, wd, wg, wu, facs, kept, ticks, slots, fold, limit):
    width, hidden = wg.shape
    experts = got.shape[0]
    hbm_spec = pl.BlockSpec(memory_space=HBM)
    arrays = [got, wd, wg, wu, *facs]
    aliases = {}
    if kept is not None:
        aliases = {1 + len(arrays) + i: 1 + i for i in range(3)}
        arrays += list(kept)
    return pl.pallas_call(
        functools.partial(backward_kernel, kept is not None, len(facs), slots, fold),
        out_shape=(
            jax.ShapeDtypeStruct((slots * fold, LANES), BF16),
            jax.ShapeDtypeStruct((ticks * slots, width), BF16),
            jax.ShapeDtypeStruct((ticks * slots, hidden), BF16),
            jax.ShapeDtypeStruct((ticks * slots, hidden), BF16),
        ),
        grid_spec=pltpu.PrefetchScalarGridSpec(
            num_scalar_prefetch=1,
            grid=(1,),
            in_specs=[pl.BlockSpec(memory_space=ANY)] + [hbm_spec] * (len(arrays) - 1),
            out_specs=(hbm_spec,) * 4,
            scratch_shapes=[
                VM((experts, slots * fold // experts, LANES), BF16),
                VM((hidden, width), BF16),
                VM((width, hidden), BF16),
                VM((width, hidden), BF16),
                VM((2, slots, hidden), F32),
                VM((slots * fold, LANES), F32),
                VM((slots, width), BF16),
                VM((slots, hidden), BF16),
                VM((slots, hidden), BF16),
                VM((slots * fold, LANES), BF16),
                pltpu.SemaphoreType.DMA((10,)),
            ],
        ),
        input_output_aliases=aliases,
        compiler_params=pltpu.CompilerParams(vmem_limit_bytes=limit),
        cost_estimate=estimate(6 * slots * width * hidden, 12e6),
        name="backward",
    )(info, *arrays)


def tables(ids, weights, experts, capacity):
    ticks, rows, top = ids.shape
    flat = ids.reshape(ticks, rows * top)
    order = jnp.arange(rows * top, dtype=jnp.int32)
    same = (flat[:, :, None] == flat[:, None, :]) & (order[None, :] < order[:, None])[None]
    target = flat * capacity + same.astype(jnp.int32).sum(axis=2)
    places = jnp.arange(experts * capacity, dtype=jnp.int32)
    chosen = places[None, :, None] == target[:, None, :]
    source = jnp.where(chosen, (order // top)[None, None, :], 0).sum(axis=2)
    scale = jnp.where(chosen, weights.reshape(ticks, 1, rows * top), 0.0).sum(axis=2)
    return target.reshape(-1), source.reshape(-1), scale.reshape(-1)


def inverse_root_steps(curvature, iterations):
    mul = functools.partial(jnp.dot, precision=lax.Precision.HIGH)
    identity_m = jnp.eye(curvature.shape[0], dtype=F32)
    frobenius = jnp.sqrt(jnp.sum(curvature * curvature))
    current = curvature / frobenius
    result = None
    for turn in range(iterations):
        factor = (5.0 * identity_m - current) * 0.25
        if result is None:
            result = factor * frobenius ** (-0.25)
        else:
            result = mul(result, factor)
        if turn < iterations - 1:
            square = mul(factor, factor)
            fourth = mul(square, square)
            current = mul(fourth, current)
    return result


def shards(section_inputs, cotangent, expert_ids, route_weights, w_gate, w_up, w_down):
    section = lax.axis_index("section")
    sections = lax.axis_size("section")
    experts = lax.axis_size("expert")
    _, ticks, rows, width = section_inputs.shape
    fold = width // LANES
    capacity = max(2, 3 * rows // experts)
    slots = experts * capacity
    wg, wu, wd = w_gate[0, 0], w_up[0, 0], w_down[0, 0]
    hidden = wg.shape[1]

    slot, src, scale = tables(expert_ids[0], route_weights[0], experts, capacity)
    x_rows = section_inputs[0]

    def exchange(value):
        return lax.all_to_all(
            value.reshape(experts, -1, LANES), "expert", split_axis=0, concat_axis=0, tiled=True
        )

    def send(info, tops, inc, plain):
        return exchange(dispatch(info, src, scale, tops, inc, plain, rows, slots, fold, capacity))

    steps = sections - 1 + ticks
    start = sections - 1 - section
    is_top = (section == sections - 1).astype(jnp.int32)
    infos = []
    for step in range(steps):
        offset = step - start
        active = ((offset >= 0) & (offset < ticks)).astype(jnp.int32)
        infos.append(jnp.stack([jnp.clip(offset, 0, ticks - 1), is_top, active]).astype(jnp.int32))

    xs_all, hiddens, facs = None, [], []
    both = exchange(first_dispatch(src, scale, x_rows, cotangent, rows, slots, fold, capacity))
    got_x = {0: both}
    kept, results, inc = None, None, None
    for step in range(steps):
        info = infos[step]
        tops = cotangent if step < ticks else None
        got = send(info, tops, inc, False) if step else both
        limit = LIMITS["backward"] if step else LIMITS["first"]
        if step < ticks:
            xs_all, hid, fac = forward(got_x[step], wg, wu, xs_all, step, ticks, slots, fold, LIMITS["forward"] if step else limit)
            hiddens.append(hid)
            facs.append(fac)
        sent, *kept = backward(info, got, wd, wg, wu, facs, kept, ticks, slots, fold, limit)
        came = exchange(sent).reshape(slots * fold, LANES)
        if step < steps - 1:
            new = combine(info, slot, tops, inc, came, rows, slots, fold)
            results = keep_rows(info, new, results, ticks, rows, fold)
            inc = lax.ppermute(new, "section", [(s, s - 1) for s in range(1, sections)])
            inc, results = lax.optimization_barrier((inc, results))
        else:
            results = combine(info, slot, tops, inc, came, rows, slots, fold, results)
        if step + 1 < ticks:
            got_x[step + 1] = send(jnp.array([step + 1, 1, 1], jnp.int32), x_rows, None, True)

    hid_all = jnp.concatenate(hiddens, axis=0)
    gram = dot(hid_all, hid_all, 0, 0)
    curvature = gram * (hidden / (jnp.trace(gram) + epsilon)) + damping * jnp.eye(
        hidden, dtype=F32
    )
    root = inverse_root_steps(curvature, NS_ITERS)
    lead = lax.dot_general(
        root,
        hid_all.astype(F32),
        (((1,), (1,)), ((), ())),
        precision=lax.Precision.HIGH,
        preferred_element_type=F32,
    )
    gs, dg, du = kept
    grad_gate, grad_up, precond = gradients(lead.astype(BF16), dg, du, xs_all, gs)
    return (results[None], grad_gate[None, None], grad_up[None, None], precond[None, None])


def solution(mesh):
    return jax.shard_map(
        shards,
        mesh=mesh,
        in_specs=(
            P("section", None, "expert", None),
            P(None, "expert", None),
            P("section", None, "expert", None),
            P("section", None, "expert", None),
            P("section", "expert", None, None),
            P("section", "expert", None, None),
            P("section", "expert", None, None),
        ),
        out_specs=(
            P("section", None, "expert", None),
            P("section", "expert", None, None),
            P("section", "expert", None, None),
            P("section", "expert", None, None),
        ),
        check_vma=False,
    )
```

```python
import functools

import jax
import jax.numpy as jnp
from jax import lax
from jax.experimental import pallas as pl
from jax.experimental.pallas import tpu as pltpu
from jax.sharding import PartitionSpec as P

NS_ITERS = 5

damping = 0.1
epsilon = 1e-06

LANES = 128
F32 = jnp.float32
BF16 = jnp.bfloat16
VM = pltpu.VMEM
SM = pltpu.SMEM
PARAMS = pltpu.CompilerParams(vmem_limit_bytes=60 << 20)
LIMITS = {"root": 62000000, "dispatch": 55000000, "backward": 55000000, "combine": 54000000, "first": 53500000, "forward": 62000000}


def estimate(flops, moved):
    return pl.CostEstimate(flops=int(flops), bytes_accessed=int(moved), transcendentals=0)


def dot(a, b, ad, bd):
    return lax.dot_general(a, b, (((ad,), (bd,)), ((), ())), preferred_element_type=F32)


HBM = pltpu.HBM
ANY = pl.ANY


def lanes_of(part):
    return pl.ds(pl.multiple_of(part * LANES, LANES), LANES)


def fold_rows(flat_ref, cur_ref, rows, fold):
    def some(part, carry):
        cur_ref[pl.ds(part, rows, stride=fold), :] = flat_ref[:, lanes_of(part)].astype(F32)
        return carry

    lax.fori_loop(0, fold, some, 0)


def flatten_rows(cur_ref, flat_ref, rows, fold):
    def some(part, carry):
        flat_ref[:, lanes_of(part)] = cur_ref[pl.ds(part, rows, stride=fold), :].astype(BF16)
        return carry

    lax.fori_loop(0, fold, some, 0)


def widen(got_ref, cur_ref, group):
    count, depth, _ = got_ref.shape

    def some(step, carry):
        part = got_ref[pl.ds(step * group, group)].astype(F32)
        here = pl.ds(pl.multiple_of(step * group * depth, group * depth), group * depth)
        cur_ref[here, :] = part.reshape(group * depth, LANES)
        return carry

    lax.fori_loop(0, count // group, some, 0)


def narrow(cur_ref, out_ref, begin, end, size):
    def some(step, carry):
        here = pl.ds(pl.multiple_of(step * size, size), size)
        out_ref[here, :] = cur_ref[here, :].astype(BF16)
        return carry

    lax.fori_loop(begin // size, end // size, some, 0)


def load_current(info_ref, top_ref, inc_ref, flat_ref, buf_ref, cur_ref, sem, rows, fold):
    def from_top():
        copy = pltpu.make_async_copy(top_ref.at[info_ref[0]], flat_ref, sem)
        copy.start()
        copy.wait()
        fold_rows(flat_ref, cur_ref, rows, fold)

    def from_above():
        copy = pltpu.make_async_copy(inc_ref, buf_ref, sem)
        copy.start()
        copy.wait()
        cur_ref[...] = buf_ref[...].astype(F32)

    if inc_ref is None:
        from_top()
    elif top_ref is None:
        from_above()
    else:
        pl.when(info_ref[1] == 1)(from_top)
        pl.when(info_ref[1] == 0)(from_above)


def place_rows(
    src_ref, scale_ref, plain, base, first, count, fold, group, stride, offset, cur_ref, out_ref
):
    def some(step, carry):
        for part in range(group):
            place = step * group + part
            row = src_ref[base + place]
            factor = scale_ref[base + place]
            if plain:
                factor = jnp.where(factor > 0.0, 1.0, 0.0)
            tile = cur_ref[pl.ds(pl.multiple_of(row * fold, fold), fold), :]
            out_ref[pl.ds(pl.multiple_of((step * stride + offset + part) * fold, fold), fold), :] = (
                tile * factor
            ).astype(BF16)
        return carry

    lax.fori_loop(first // group, (first + count) // group, some, 0)


CHUNKS = 2


def dispatch_kernel(
    has_top, has_inc, plain, rows, slots, fold, group, info_ref, src_ref, scale_ref, *refs
):
    refs = list(refs)
    top_ref = refs.pop(0) if has_top else None
    inc_ref = refs.pop(0) if has_inc else None
    out_ref, flat_ref, buf_ref, cur_ref, put_ref, sems = refs
    load_current(info_ref, top_ref, inc_ref, flat_ref, buf_ref, cur_ref, sems.at[0], rows, fold)
    base = info_ref[0] * slots
    count = slots // CHUNKS
    copies = []
    for chunk in range(CHUNKS):
        place_rows(
            src_ref, scale_ref, plain, base, chunk * count, count, fold, group, group, 0,
            cur_ref, put_ref,
        )
        part = pl.ds(chunk * count * fold, count * fold)
        copies.append(
            pltpu.make_async_copy(put_ref.at[part], out_ref.at[part], sems.at[1 + chunk])
        )
        copies[-1].start()
    for copy in copies:
        copy.wait()


def dispatch(info, src, scale, top, inc, plain, rows, slots, fold, group):
    arrays = [value for value in (top, inc) if value is not None]
    return pl.pallas_call(
        functools.partial(
            dispatch_kernel, top is not None, inc is not None, plain, rows, slots, fold, group
        ),
        out_shape=jax.ShapeDtypeStruct((slots * fold, LANES), BF16),
        grid_spec=pltpu.PrefetchScalarGridSpec(
            num_scalar_prefetch=2,
            grid=(1,),
            in_specs=[pl.BlockSpec(memory_space=SM)]
            + [pl.BlockSpec(memory_space=HBM)] * (top is not None)
            + [pl.BlockSpec(memory_space=ANY)] * (inc is not None),
            out_specs=pl.BlockSpec(memory_space=HBM),
            scratch_shapes=[
                VM((rows, fold * LANES), BF16),
                VM((rows * fold, LANES), BF16),
                VM((rows * fold, LANES), F32),
                VM((slots * fold, LANES), BF16),
                pltpu.SemaphoreType.DMA((1 + CHUNKS,)),
            ],
        ),
        compiler_params=pltpu.CompilerParams(vmem_limit_bytes=LIMITS["dispatch"]),
        cost_estimate=estimate(1e6, 4e6),
        name="dispatch",
    )(info, src, scale, *arrays)


def first_kernel(rows, slots, fold, group, src_ref, scale_ref, x_ref, top_ref, out_ref, *rest):
    buf_x, buf_g, cur_x, cur_g, put_ref, sems = rest
    copies = [
        pltpu.make_async_copy(x_ref.at[0], buf_x, sems.at[0]),
        pltpu.make_async_copy(top_ref.at[0], buf_g, sems.at[1]),
    ]
    for copy in copies:
        copy.start()
    copies[0].wait()
    fold_rows(buf_x, cur_x, rows, fold)
    copies[1].wait()
    fold_rows(buf_g, cur_g, rows, fold)
    count = slots // CHUNKS
    copies = []
    for chunk in range(CHUNKS):
        for offset, plain, cur in ((0, True, cur_x), (group, False, cur_g)):
            place_rows(
                src_ref, scale_ref, plain, 0, chunk * count, count, fold, group, 2 * group, offset,
                cur, put_ref,
            )
        part = pl.ds(chunk * count * fold * 2, count * fold * 2)
        copies.append(
            pltpu.make_async_copy(put_ref.at[part], out_ref.at[part], sems.at[2 + chunk])
        )
        copies[-1].start()
    for copy in copies:
        copy.wait()


def first_dispatch(src, scale, x, top, rows, slots, fold, group):
    return pl.pallas_call(
        functools.partial(first_kernel, rows, slots, fold, group),
        out_shape=jax.ShapeDtypeStruct((2 * slots * fold, LANES), BF16),
        in_specs=[pl.BlockSpec(memory_space=SM)] * 2 + [pl.BlockSpec(memory_space=HBM)] * 2,
        out_specs=pl.BlockSpec(memory_space=HBM),
        scratch_shapes=[VM((rows, fold * LANES), BF16)] * 2
        + [VM((rows * fold, LANES), F32)] * 2
        + [VM((2 * slots * fold, LANES), BF16), pltpu.SemaphoreType.DMA((2 + CHUNKS,))],
        compiler_params=PARAMS,
        cost_estimate=estimate(1e6, 4e6),
        name="first_dispatch",
    )(src, scale, x, top)


def combine_kernel(has_top, has_inc, last, rows, fold, info_ref, slot_ref, *refs):
    refs = list(refs)
    top_ref = refs.pop(0) if has_top else None
    inc_ref = refs.pop(0) if has_inc else None
    came_hbm = refs.pop(0)
    if last:
        old_ref, flat_ref, top_buf, buf_ref, cur_ref, came_ref, sems = refs
    else:
        new_ref, top_buf, buf_ref, cur_ref, came_ref, sems = refs
    came_copy = pltpu.make_async_copy(came_hbm, came_ref, sems.at[1])
    came_copy.start()
    load_current(info_ref, top_ref, inc_ref, top_buf, buf_ref, cur_ref, sems.at[0], rows, fold)
    came_copy.wait()
    base = info_ref[0] * rows * 2

    def some(step, carry):
        for part in range(4):
            row = step * 4 + part
            first = slot_ref[base + 2 * row]
            second = slot_ref[base + 2 * row + 1]
            here = pl.ds(pl.multiple_of(row * fold, fold), fold)
            one = came_ref[pl.ds(pl.multiple_of(first * fold, fold), fold), :].astype(F32)
            two = came_ref[pl.ds(pl.multiple_of(second * fold, fold), fold), :].astype(F32)
            total = cur_ref[here, :] + (one + two)
            if last:
                cur_ref[here, :] = total
            else:
                buf_ref[here, :] = total.astype(BF16)
        return carry

    if not last:
        half = rows // 2
        copies = []
        for chunk in range(2):
            lax.fori_loop(chunk * half // 4, (chunk + 1) * half // 4, some, 0)
            part = pl.ds(chunk * half * fold, half * fold)
            copies.append(
                pltpu.make_async_copy(buf_ref.at[part], new_ref.at[part], sems.at[2 + chunk])
            )
            copies[-1].start()
        for copy in copies:
            copy.wait()
    else:
        lax.fori_loop(0, rows // 4, some, 0)
        unfold_rows(info_ref, cur_ref, old_ref, flat_ref, rows, fold)


def unfold_rows(info_ref, cur_ref, old_ref, flat_ref, rows, fold):
    @pl.when(info_ref[2] == 1)
    def _():
        flatten_rows(cur_ref, flat_ref.at[0], rows, fold)

    @pl.when(info_ref[2] == 0)
    def _():
        flat_ref[...] = old_ref[...]


def combine(info, slot, top, inc, came, rows, slots, fold, results=None):
    last = results is not None
    arrays = [value for value in (top, inc, came) if value is not None]
    specs = [pl.BlockSpec(memory_space=HBM)] * (top is not None)
    specs += [pl.BlockSpec(memory_space=ANY)] * (len(arrays) - len(specs))
    aliases = {}
    out_shape = jax.ShapeDtypeStruct((rows * fold, LANES), BF16)
    out_specs = pl.BlockSpec(memory_space=HBM)
    if last:
        block = pl.BlockSpec((1, rows, fold * LANES), lambda i, info, *_: (info[0], 0, 0))
        aliases = {2 + len(arrays): 0}
        out_shape = jax.ShapeDtypeStruct(results.shape, BF16)
        arrays, specs, out_specs = arrays + [results], specs + [block], block
    return pl.pallas_call(
        functools.partial(combine_kernel, top is not None, inc is not None, last, rows, fold),
        out_shape=out_shape,
        grid_spec=pltpu.PrefetchScalarGridSpec(
            num_scalar_prefetch=2,
            grid=(1,),
            in_specs=specs,
            out_specs=out_specs,
            scratch_shapes=[
                VM((rows, fold * LANES), BF16),
                VM((rows * fold, LANES), BF16),
                VM((rows * fold, LANES), F32),
                VM((slots * fold, LANES), BF16),
                pltpu.SemaphoreType.DMA((4,)),
            ],
        ),
        input_output_aliases=aliases,
        compiler_params=pltpu.CompilerParams(vmem_limit_bytes=LIMITS["combine"]),
        cost_estimate=estimate(1e6, 4e6),
        name="combine",
    )(info, slot, *arrays)


def keep_kernel(rows, fold, aliased, info_ref, new_ref, *refs):
    old_ref, flat_ref, cur_ref = refs if aliased else (None, *refs)
    cur_ref[...] = new_ref[...].astype(F32)
    if aliased:
        unfold_rows(info_ref, cur_ref, old_ref, flat_ref, rows, fold)
    else:
        flatten_rows(cur_ref, flat_ref.at[0], rows, fold)


def keep_rows(info, new, results, ticks, rows, fold):
    block = pl.BlockSpec((1, rows, fold * LANES), lambda i, info: (info[0], 0, 0))
    more = [] if results is None else [results]
    return pl.pallas_call(
        functools.partial(keep_kernel, rows, fold, results is not None),
        out_shape=jax.ShapeDtypeStruct((ticks, rows, fold * LANES), BF16),
        grid_spec=pltpu.PrefetchScalarGridSpec(
            num_scalar_prefetch=1,
            grid=(1,),
            in_specs=[pl.BlockSpec((rows * fold, LANES), lambda i, info: (0, 0))] + [block] * len(more),
            out_specs=block,
            scratch_shapes=[VM((rows * fold, LANES), F32)],
        ),
        input_output_aliases={2: 0} if more else {},
        compiler_params=PARAMS,
        cost_estimate=estimate(1e6, 1e6),
        name="keep_rows",
    )(info, new, *more)


def gradients_kernel(lead_ref, dg_ref, du_ref, xs_ref, gs_ref, gate_ref, up_ref, down_ref):
    rows_x = xs_ref[...]
    gate_ref[...] = dot(rows_x, dg_ref[...], 0, 0)
    up_ref[...] = dot(rows_x, du_ref[...], 0, 0)
    down_ref[...] = dot(lead_ref[...], gs_ref[...], 1, 0)


def gradients(lead, dg, du, xs, gs):
    depth, width = xs.shape
    hidden = dg.shape[1]
    wide = 256

    def whole(value):
        return pl.BlockSpec(value.shape, lambda i: (0, 0))

    columns = pl.BlockSpec((depth, wide), lambda i: (0, i))
    rows_out = pl.BlockSpec((wide, hidden), lambda i: (i, 0))
    return pl.pallas_call(
        gradients_kernel,
        out_shape=(
            jax.ShapeDtypeStruct((width, hidden), F32),
            jax.ShapeDtypeStruct((width, hidden), F32),
            jax.ShapeDtypeStruct((hidden, width), F32),
        ),
        grid=(width // wide,),
        in_specs=[whole(lead), whole(dg), whole(du), columns, columns],
        out_specs=(rows_out, rows_out, pl.BlockSpec((hidden, wide), lambda i: (0, i))),
        compiler_params=PARAMS,
        cost_estimate=estimate(6 * hidden * width * depth, 18e6),
        name="gradients",
    )(lead, dg, du, xs, gs)


def forward_kernel(aliased, tick, slots, fold, experts, got_hbm, wg_hbm, wu_hbm, *refs):
    refs = list(refs)
    if aliased:
        refs.pop(0)
    xs_hbm, hid_hbm, fac_hbm, got, both_w, scr, xs, hid, fac, sems = refs
    copies = [
        pltpu.make_async_copy(got_hbm.at[:, pl.ds(0, got.shape[1])], got, sems.at[0]),
        pltpu.make_async_copy(wg_hbm, both_w.at[0], sems.at[1]),
        pltpu.make_async_copy(wu_hbm, both_w.at[1], sems.at[2]),
    ]
    for copy in copies:
        copy.start()
    copies[0].wait()
    widen(got, scr, 4)
    flatten_rows(scr, xs, slots, fold)
    puts = [
        pltpu.make_async_copy(xs, xs_hbm.at[pl.ds(tick * slots, slots)], sems.at[3]),
        pltpu.make_async_copy(hid, hid_hbm, sems.at[4]),
        pltpu.make_async_copy(fac, fac_hbm, sems.at[5]),
    ]
    puts[0].start()
    copies[1].wait()
    copies[2].wait()

    def project(which, carry):
        fac[which] = dot(xs[...], both_w[which], 1, 0)
        return carry

    lax.fori_loop(0, 2, project, 0)
    gate, up = fac[0], fac[1]
    logistic = jax.nn.sigmoid(gate)
    soft = gate * logistic
    fac[0] = up * (logistic * (1.0 + gate * (1.0 - logistic)))
    fac[1] = soft
    puts[2].start()
    hid[...] = (soft * up).astype(BF16)
    puts[1].start()
    for put in puts:
        put.wait()


def forward(got, wg, wu, xs_all, tick, ticks, slots, fold, limit):
    experts = got.shape[0]
    width, hidden = wg.shape
    arrays = [got, wg, wu]
    aliases = {}
    if xs_all is not None:
        arrays.append(xs_all)
        aliases = {3: 0}
    hbm_spec = pl.BlockSpec(memory_space=HBM)
    return pl.pallas_call(
        functools.partial(forward_kernel, xs_all is not None, tick, slots, fold, experts),
        out_shape=(
            jax.ShapeDtypeStruct((ticks * slots, width), BF16),
            jax.ShapeDtypeStruct((slots, hidden), BF16),
            jax.ShapeDtypeStruct((2, slots, hidden), F32),
        ),
        in_specs=[pl.BlockSpec(memory_space=ANY)] + [hbm_spec] * (len(arrays) - 1),
        out_specs=(hbm_spec,) * 3,
        scratch_shapes=[
            VM((experts, slots * fold // experts, LANES), BF16),
            VM((2, width, hidden), BF16),
            VM((slots * fold, LANES), F32),
            VM((slots, width), BF16),
            VM((slots, hidden), BF16),
            VM((2, slots, hidden), F32),
            pltpu.SemaphoreType.DMA((6,)),
        ],
        input_output_aliases=aliases,
        compiler_params=pltpu.CompilerParams(vmem_limit_bytes=limit),
        cost_estimate=estimate(4 * slots * width * hidden, 8e6),
        name="forward",
    )(*arrays)


def backward_kernel(
    aliased, count, slots, fold, info_ref, got_hbm, wd_hbm, wg_hbm, wu_hbm, *refs
):
    refs = list(refs)
    fac_hbm = refs[:count]
    del refs[:count]
    if aliased:
        del refs[:3]
    out_hbm, gs_hbm, dg_hbm, du_hbm, got, wd, wg, wu, fac, scr, gs, dg, du, out, sems = refs
    begin = got_hbm.shape[1] - got.shape[1]
    copies = [
        pltpu.make_async_copy(got_hbm.at[:, pl.ds(begin, got.shape[1])], got, sems.at[0]),
        pltpu.make_async_copy(wd_hbm, wd, sems.at[1]),
        pltpu.make_async_copy(wg_hbm, wg, sems.at[2]),
        pltpu.make_async_copy(wu_hbm, wu, sems.at[3]),
    ]
    copies[0].start()
    copies[1].start()
    for which in range(count):

        @pl.when(info_ref[0] == which)
        def _(which=which):
            pltpu.make_async_copy(fac_hbm[which], fac, sems.at[4]).start()

    copies[2].start()
    copies[3].start()
    copies[0].wait()
    widen(got, scr, 4)
    flatten_rows(scr, gs, slots, fold)
    mine = pl.ds(pl.multiple_of(info_ref[0] * slots, slots), slots)
    keeps = [
        pltpu.make_async_copy(gs, gs_hbm.at[mine], sems.at[5]),
        pltpu.make_async_copy(dg, dg_hbm.at[mine], sems.at[6]),
        pltpu.make_async_copy(du, du_hbm.at[mine], sems.at[7]),
    ]
    copies[1].wait()
    grad_hidden = dot(gs[...], wd[...], 1, 1)
    pltpu.make_async_copy(fac_hbm[0], fac, sems.at[4]).wait()
    d_gate = (grad_hidden * fac[0]).astype(BF16)
    d_up = (grad_hidden * fac[1]).astype(BF16)
    dg[...] = d_gate
    du[...] = d_up
    copies[2].wait()
    copies[3].wait()

    @pl.when(info_ref[2] == 1)
    def _():
        for keep in keeps:
            keep.start()

    puts = []
    wide = 4
    for part in range(0, fold, wide):
        cols = slice(part * LANES, (part + wide) * LANES)
        back = dot(d_gate, wg[cols, :], 1, 1) + dot(d_up, wu[cols, :], 1, 1)
        for inner in range(wide):
            scr[pl.ds(part + inner, slots, stride=fold), :] = back[
                :, inner * LANES : (inner + 1) * LANES
            ]
    size = slots * fold // 2
    for chunk in range(2):
        some = pl.ds(chunk * size, size)
        narrow(scr, out, chunk * size, (chunk + 1) * size, 256)
        puts.append(pltpu.make_async_copy(out.at[some], out_hbm.at[some], sems.at[8 + chunk]))
        puts[-1].start()
    for put in puts:
        put.wait()

    @pl.when(info_ref[2] == 1)
    def _():
        for keep in keeps:
            keep.wait()


def backward(info, got, wd, wg, wu, facs, kept, ticks, slots, fold, limit):
    width, hidden = wg.shape
    experts = got.shape[0]
    hbm_spec = pl.BlockSpec(memory_space=HBM)
    arrays = [got, wd, wg, wu, *facs]
    aliases = {}
    if kept is not None:
        aliases = {1 + len(arrays) + i: 1 + i for i in range(3)}
        arrays += list(kept)
    return pl.pallas_call(
        functools.partial(backward_kernel, kept is not None, len(facs), slots, fold),
        out_shape=(
            jax.ShapeDtypeStruct((slots * fold, LANES), BF16),
            jax.ShapeDtypeStruct((ticks * slots, width), BF16),
            jax.ShapeDtypeStruct((ticks * slots, hidden), BF16),
            jax.ShapeDtypeStruct((ticks * slots, hidden), BF16),
        ),
        grid_spec=pltpu.PrefetchScalarGridSpec(
            num_scalar_prefetch=1,
            grid=(1,),
            in_specs=[pl.BlockSpec(memory_space=ANY)] + [hbm_spec] * (len(arrays) - 1),
            out_specs=(hbm_spec,) * 4,
            scratch_shapes=[
                VM((experts, slots * fold // experts, LANES), BF16),
                VM((hidden, width), BF16),
                VM((width, hidden), BF16),
                VM((width, hidden), BF16),
                VM((2, slots, hidden), F32),
                VM((slots * fold, LANES), F32),
                VM((slots, width), BF16),
                VM((slots, hidden), BF16),
                VM((slots, hidden), BF16),
                VM((slots * fold, LANES), BF16),
                pltpu.SemaphoreType.DMA((10,)),
            ],
        ),
        input_output_aliases=aliases,
        compiler_params=pltpu.CompilerParams(vmem_limit_bytes=limit),
        cost_estimate=estimate(6 * slots * width * hidden, 12e6),
        name="backward",
    )(info, *arrays)


def tables(ids, weights, experts, capacity):
    ticks, rows, top = ids.shape
    flat = ids.reshape(ticks, rows * top)
    order = jnp.arange(rows * top, dtype=jnp.int32)
    same = (flat[:, :, None] == flat[:, None, :]) & (order[None, :] < order[:, None])[None]
    target = flat * capacity + same.astype(jnp.int32).sum(axis=2)
    places = jnp.arange(experts * capacity, dtype=jnp.int32)
    chosen = places[None, :, None] == target[:, None, :]
    source = jnp.where(chosen, (order // top)[None, None, :], 0).sum(axis=2)
    scale = jnp.where(chosen, weights.reshape(ticks, 1, rows * top), 0.0).sum(axis=2)
    return target.reshape(-1), source.reshape(-1), scale.reshape(-1)


def split(value):
    high = value.astype(BF16)
    return high, (value - high.astype(F32)).astype(BF16)


def mul(a, b):
    a_high, a_low = split(a)
    b_high, b_low = split(b)
    return dot(a_high, b_high, 1, 0) + (dot(a_high, b_low, 1, 0) + dot(a_low, b_high, 1, 0))


def eye_like(value):
    rows = lax.broadcasted_iota(jnp.int32, value.shape, 0)
    return jnp.where(rows == lax.broadcasted_iota(jnp.int32, value.shape, 1), 1.0, 0.0)


def total_of(value):
    return jnp.sum(jnp.sum(value, axis=1, keepdims=True), axis=0, keepdims=True)


RES, FACTOR, CURRENT = 0, 1, 4


def root_turns(buf_ref, turns):
    def product(step, carry):
        right = jnp.where(step == 0, FACTOR, jnp.where(step == 3, CURRENT, step))
        to = jnp.where(step == 0, RES, step + 1)
        buf_ref[to] = mul(buf_ref[step], buf_ref[right])
        return carry

    def turn(_, carry):
        current = buf_ref[CURRENT]
        buf_ref[FACTOR] = (5.0 * eye_like(current) - current) * 0.25
        return lax.fori_loop(0, 4, product, carry)

    lax.fori_loop(0, turns, turn, 0)


def root_start_kernel(count, turns, *refs):
    state_ref, buf_ref = refs[count:]
    gram = None
    for ref in refs[:count]:
        term = dot(ref[...], ref[...], 0, 0)
        gram = term if gram is None else gram + term
    identity_m = eye_like(gram)
    ratio = gram.shape[0] / (total_of(gram * identity_m) + epsilon)
    curvature = gram * ratio + damping * identity_m
    frobenius = jnp.sqrt(total_of(curvature * curvature))
    buf_ref[CURRENT] = curvature * (1.0 / frobenius)
    buf_ref[RES] = identity_m * lax.rsqrt(jnp.sqrt(frobenius))
    root_turns(buf_ref, turns)
    state_ref[0] = buf_ref[RES]
    state_ref[1] = buf_ref[CURRENT]


def root_more_kernel(turns, state_in, state_ref, buf_ref):
    buf_ref[RES] = state_in[0]
    buf_ref[CURRENT] = state_in[1]
    root_turns(buf_ref, turns)
    state_ref[0] = buf_ref[RES]
    state_ref[1] = buf_ref[CURRENT]


def root_end_kernel(count, state_in, *refs):
    lead_ref, root_ref = refs[count:]
    current = state_in[1]
    root_ref[...] = mul(state_in[0], (5.0 * eye_like(current) - current) * 0.25)
    high, low = split(root_ref[...])
    width = refs[0].shape[0]
    for which, ref in enumerate(refs[:count]):
        lead = dot(high, ref[...], 1, 1) + dot(low, ref[...], 1, 1)
        lead_ref[:, which * width : (which + 1) * width] = lead.astype(BF16)


def root_call(kernel, name, out_shape, flops, scratch, *arrays):
    whole = pl.BlockSpec(memory_space=pltpu.VMEM)
    return pl.pallas_call(
        kernel,
        out_shape=out_shape,
        in_specs=[whole] * len(arrays),
        out_specs=whole,
        scratch_shapes=[scratch],
        compiler_params=pltpu.CompilerParams(vmem_limit_bytes=LIMITS["root"]),
        cost_estimate=estimate(flops, 4e6),
        name=name,
    )(*arrays)


def shards(section_inputs, cotangent, expert_ids, route_weights, w_gate, w_up, w_down):
    section = lax.axis_index("section")
    sections = lax.axis_size("section")
    experts = lax.axis_size("expert")
    _, ticks, rows, width = section_inputs.shape
    fold = width // LANES
    capacity = max(2, 3 * rows // experts)
    slots = experts * capacity
    wg, wu, wd = w_gate[0, 0], w_up[0, 0], w_down[0, 0]
    hidden = wg.shape[1]

    slot, src, scale = tables(expert_ids[0], route_weights[0], experts, capacity)
    x_rows = section_inputs[0]

    def exchange(value):
        return lax.all_to_all(
            value.reshape(experts, -1, LANES), "expert", split_axis=0, concat_axis=0, tiled=True
        )

    def send(info, tops, inc, plain):
        return exchange(dispatch(info, src, scale, tops, inc, plain, rows, slots, fold, capacity))

    steps = sections - 1 + ticks
    start = sections - 1 - section
    is_top = (section == sections - 1).astype(jnp.int32)
    infos = []
    for step in range(steps):
        offset = step - start
        active = ((offset >= 0) & (offset < ticks)).astype(jnp.int32)
        infos.append(jnp.stack([jnp.clip(offset, 0, ticks - 1), is_top, active]).astype(jnp.int32))

    xs_all, hiddens, facs = None, [], []
    pair = jax.ShapeDtypeStruct((2, hidden, hidden), F32)
    work = VM((5, hidden, hidden), F32)
    product = 6 * hidden**3

    def root_part(part, beside):
        if part == 0:
            kernel = functools.partial(root_start_kernel, ticks, 2)
            value = root_call(kernel, "root_start", pair, 8 * product, work, *hiddens)
        elif part == 1:
            kernel = functools.partial(root_more_kernel, NS_ITERS - 3)
            value = root_call(kernel, "root_more", pair, 8 * product, work, state)
        else:
            shape = jax.ShapeDtypeStruct((hidden, ticks * slots), BF16)
            kernel = functools.partial(root_end_kernel, ticks)
            one = VM((hidden, hidden), F32)
            value = root_call(kernel, "root_end", shape, 3 * product, one, state, *hiddens)
        return lax.optimization_barrier((beside, value))

    both = exchange(first_dispatch(src, scale, x_rows, cotangent, rows, slots, fold, capacity))
    got_x = {0: both}
    kept, results, inc = None, None, None
    for step in range(steps):
        info = infos[step]
        tops = cotangent if step < ticks else None
        got = send(info, tops, inc, False) if step else both
        limit = LIMITS["backward"] if step else LIMITS["first"]
        if step < ticks:
            xs_all, hid, fac = forward(got_x[step], wg, wu, xs_all, step, ticks, slots, fold, LIMITS["forward"] if step else limit)
            hiddens.append(hid)
            facs.append(fac)
        if step == ticks:
            got, state = root_part(1, got)
        sent, *kept = backward(info, got, wd, wg, wu, facs, kept, ticks, slots, fold, limit)
        came = exchange(sent).reshape(slots * fold, LANES)
        if step == ticks - 1:
            came, state = root_part(0, came)
        if step == ticks:
            came, lead = root_part(2, came)
        if step < steps - 1:
            new = combine(info, slot, tops, inc, came, rows, slots, fold)
            results = keep_rows(info, new, results, ticks, rows, fold)
            inc = lax.ppermute(new, "section", [(s, s - 1) for s in range(1, sections)])
            inc, results = lax.optimization_barrier((inc, results))
        else:
            results = combine(info, slot, tops, inc, came, rows, slots, fold, results)
        if step + 1 < ticks:
            got_x[step + 1] = send(jnp.array([step + 1, 1, 1], jnp.int32), x_rows, None, True)

    gs, dg, du = kept
    grad_gate, grad_up, precond = gradients(lead, dg, du, xs_all, gs)
    return (results[None], grad_gate[None, None], grad_up[None, None], precond[None, None])


def solution(mesh):
    return jax.shard_map(
        shards,
        mesh=mesh,
        in_specs=(
            P("section", None, "expert", None),
            P(None, "expert", None),
            P("section", None, "expert", None),
            P("section", None, "expert", None),
            P("section", "expert", None, None),
            P("section", "expert", None, None),
            P("section", "expert", None, None),
        ),
        out_specs=(
            P("section", None, "expert", None),
            P("section", "expert", None, None),
            P("section", "expert", None, None),
            P("section", "expert", None, None),
        ),
        check_vma=False,
    )
```

```python
import functools

import jax
import jax.numpy as jnp
from jax import lax
from jax.experimental import pallas as pl
from jax.experimental.pallas import tpu as pltpu
from jax.sharding import PartitionSpec as P

NS_ITERS = 5

damping = 0.1
epsilon = 1e-06

LANES = 128
F32 = jnp.float32
BF16 = jnp.bfloat16
VM = pltpu.VMEM
SM = pltpu.SMEM
PARAMS = pltpu.CompilerParams(vmem_limit_bytes=60 << 20)
LIMITS = {"root": 62000000, "dispatch": 55000000, "backward": 53500000, "combine": 54000000, "first": 53500000, "forward": 62000000}


def estimate(flops, moved):
    return pl.CostEstimate(flops=int(flops), bytes_accessed=int(moved), transcendentals=0)


def dot(a, b, ad, bd):
    return lax.dot_general(a, b, (((ad,), (bd,)), ((), ())), preferred_element_type=F32)


HBM = pltpu.HBM
ANY = pl.ANY


def lanes_of(part):
    return pl.ds(pl.multiple_of(part * LANES, LANES), LANES)


def fold_rows(flat_ref, cur_ref, rows, fold):
    def some(part, carry):
        cur_ref[pl.ds(part, rows, stride=fold), :] = flat_ref[:, lanes_of(part)].astype(F32)
        return carry

    lax.fori_loop(0, fold, some, 0)


def flatten_rows(cur_ref, flat_ref, rows, fold):
    def some(part, carry):
        flat_ref[:, lanes_of(part)] = cur_ref[pl.ds(part, rows, stride=fold), :].astype(BF16)
        return carry

    lax.fori_loop(0, fold, some, 0)


def widen(got_ref, cur_ref, group):
    count, depth, _ = got_ref.shape

    def some(step, carry):
        part = got_ref[pl.ds(step * group, group)].astype(F32)
        here = pl.ds(pl.multiple_of(step * group * depth, group * depth), group * depth)
        cur_ref[here, :] = part.reshape(group * depth, LANES)
        return carry

    lax.fori_loop(0, count // group, some, 0)


def narrow(cur_ref, out_ref, begin, end, size):
    def some(step, carry):
        here = pl.ds(pl.multiple_of(step * size, size), size)
        out_ref[here, :] = cur_ref[here, :].astype(BF16)
        return carry

    lax.fori_loop(begin // size, end // size, some, 0)


def load_current(info_ref, top_ref, inc_ref, flat_ref, buf_ref, cur_ref, sem, rows, fold):
    def from_top():
        copy = pltpu.make_async_copy(top_ref.at[info_ref[0]], flat_ref, sem)
        copy.start()
        copy.wait()
        fold_rows(flat_ref, cur_ref, rows, fold)

    def from_above():
        copy = pltpu.make_async_copy(inc_ref, buf_ref, sem)
        copy.start()
        copy.wait()
        cur_ref[...] = buf_ref[...].astype(F32)

    if inc_ref is None:
        from_top()
    elif top_ref is None:
        from_above()
    else:
        pl.when(info_ref[1] == 1)(from_top)
        pl.when(info_ref[1] == 0)(from_above)


def place_rows(
    src_ref, scale_ref, plain, base, first, count, fold, group, stride, offset, cur_ref, out_ref
):
    def some(step, carry):
        for part in range(group):
            place = step * group + part
            row = src_ref[base + place]
            factor = scale_ref[base + place]
            if plain:
                factor = jnp.where(factor > 0.0, 1.0, 0.0)
            tile = cur_ref[pl.ds(pl.multiple_of(row * fold, fold), fold), :]
            out_ref[pl.ds(pl.multiple_of((step * stride + offset + part) * fold, fold), fold), :] = (
                tile * factor
            ).astype(BF16)
        return carry

    lax.fori_loop(first // group, (first + count) // group, some, 0)


CHUNKS = 2


def dispatch_kernel(
    has_top, has_inc, plain, rows, slots, fold, group, info_ref, src_ref, scale_ref, *refs
):
    refs = list(refs)
    top_ref = refs.pop(0) if has_top else None
    inc_ref = refs.pop(0) if has_inc else None
    out_ref, flat_ref, buf_ref, cur_ref, put_ref, sems = refs
    load_current(info_ref, top_ref, inc_ref, flat_ref, buf_ref, cur_ref, sems.at[0], rows, fold)
    base = info_ref[0] * slots
    count = slots // CHUNKS
    copies = []
    for chunk in range(CHUNKS):
        place_rows(
            src_ref, scale_ref, plain, base, chunk * count, count, fold, group, group, 0,
            cur_ref, put_ref,
        )
        part = pl.ds(chunk * count * fold, count * fold)
        copies.append(
            pltpu.make_async_copy(put_ref.at[part], out_ref.at[part], sems.at[1 + chunk])
        )
        copies[-1].start()
    for copy in copies:
        copy.wait()


def dispatch(info, src, scale, top, inc, plain, rows, slots, fold, group):
    arrays = [value for value in (top, inc) if value is not None]
    return pl.pallas_call(
        functools.partial(
            dispatch_kernel, top is not None, inc is not None, plain, rows, slots, fold, group
        ),
        out_shape=jax.ShapeDtypeStruct((slots * fold, LANES), BF16),
        grid_spec=pltpu.PrefetchScalarGridSpec(
            num_scalar_prefetch=2,
            grid=(1,),
            in_specs=[pl.BlockSpec(memory_space=SM)]
            + [pl.BlockSpec(memory_space=HBM)] * (top is not None)
            + [pl.BlockSpec(memory_space=ANY)] * (inc is not None),
            out_specs=pl.BlockSpec(memory_space=HBM),
            scratch_shapes=[
                VM((rows, fold * LANES), BF16),
                VM((rows * fold, LANES), BF16),
                VM((rows * fold, LANES), F32),
                VM((slots * fold, LANES), BF16),
                pltpu.SemaphoreType.DMA((1 + CHUNKS,)),
            ],
        ),
        compiler_params=pltpu.CompilerParams(vmem_limit_bytes=LIMITS["dispatch"]),
        cost_estimate=estimate(1e6, 4e6),
        name="dispatch",
    )(info, src, scale, *arrays)


def first_kernel(rows, slots, fold, group, src_ref, scale_ref, x_ref, top_ref, out_ref, *rest):
    buf_x, buf_g, cur_x, cur_g, put_ref, sems = rest
    copies = [
        pltpu.make_async_copy(x_ref.at[0], buf_x, sems.at[0]),
        pltpu.make_async_copy(top_ref.at[0], buf_g, sems.at[1]),
    ]
    for copy in copies:
        copy.start()
    copies[0].wait()
    fold_rows(buf_x, cur_x, rows, fold)
    copies[1].wait()
    fold_rows(buf_g, cur_g, rows, fold)
    count = slots // CHUNKS
    copies = []
    for chunk in range(CHUNKS):
        for offset, plain, cur in ((0, True, cur_x), (group, False, cur_g)):
            place_rows(
                src_ref, scale_ref, plain, 0, chunk * count, count, fold, group, 2 * group, offset,
                cur, put_ref,
            )
        part = pl.ds(chunk * count * fold * 2, count * fold * 2)
        copies.append(
            pltpu.make_async_copy(put_ref.at[part], out_ref.at[part], sems.at[2 + chunk])
        )
        copies[-1].start()
    for copy in copies:
        copy.wait()


def first_dispatch(src, scale, x, top, rows, slots, fold, group):
    return pl.pallas_call(
        functools.partial(first_kernel, rows, slots, fold, group),
        out_shape=jax.ShapeDtypeStruct((2 * slots * fold, LANES), BF16),
        in_specs=[pl.BlockSpec(memory_space=SM)] * 2 + [pl.BlockSpec(memory_space=HBM)] * 2,
        out_specs=pl.BlockSpec(memory_space=HBM),
        scratch_shapes=[VM((rows, fold * LANES), BF16)] * 2
        + [VM((rows * fold, LANES), F32)] * 2
        + [VM((2 * slots * fold, LANES), BF16), pltpu.SemaphoreType.DMA((2 + CHUNKS,))],
        compiler_params=PARAMS,
        cost_estimate=estimate(1e6, 4e6),
        name="first_dispatch",
    )(src, scale, x, top)


def combine_kernel(has_top, has_inc, last, rows, fold, info_ref, slot_ref, *refs):
    refs = list(refs)
    top_ref = refs.pop(0) if has_top else None
    inc_ref = refs.pop(0) if has_inc else None
    came_hbm = refs.pop(0)
    if last:
        old_ref, flat_ref, top_buf, buf_ref, cur_ref, came_ref, sems = refs
    else:
        new_ref, top_buf, buf_ref, cur_ref, came_ref, sems = refs
    came_copy = pltpu.make_async_copy(came_hbm, came_ref, sems.at[1])
    came_copy.start()
    load_current(info_ref, top_ref, inc_ref, top_buf, buf_ref, cur_ref, sems.at[0], rows, fold)
    came_copy.wait()
    base = info_ref[0] * rows * 2

    def some(step, carry):
        for part in range(4):
            row = step * 4 + part
            first = slot_ref[base + 2 * row]
            second = slot_ref[base + 2 * row + 1]
            here = pl.ds(pl.multiple_of(row * fold, fold), fold)
            one = came_ref[pl.ds(pl.multiple_of(first * fold, fold), fold), :].astype(F32)
            two = came_ref[pl.ds(pl.multiple_of(second * fold, fold), fold), :].astype(F32)
            total = cur_ref[here, :] + (one + two)
            if last:
                cur_ref[here, :] = total
            else:
                buf_ref[here, :] = total.astype(BF16)
        return carry

    if not last:
        half = rows // 2
        copies = []
        for chunk in range(2):
            lax.fori_loop(chunk * half // 4, (chunk + 1) * half // 4, some, 0)
            part = pl.ds(chunk * half * fold, half * fold)
            copies.append(
                pltpu.make_async_copy(buf_ref.at[part], new_ref.at[part], sems.at[2 + chunk])
            )
            copies[-1].start()
        for copy in copies:
            copy.wait()
    else:
        lax.fori_loop(0, rows // 4, some, 0)
        unfold_rows(info_ref, cur_ref, old_ref, flat_ref, rows, fold)


def unfold_rows(info_ref, cur_ref, old_ref, flat_ref, rows, fold):
    @pl.when(info_ref[2] == 1)
    def _():
        flatten_rows(cur_ref, flat_ref.at[0], rows, fold)

    @pl.when(info_ref[2] == 0)
    def _():
        flat_ref[...] = old_ref[...]


def combine(info, slot, top, inc, came, rows, slots, fold, results=None):
    last = results is not None
    arrays = [value for value in (top, inc, came) if value is not None]
    specs = [pl.BlockSpec(memory_space=HBM)] * (top is not None)
    specs += [pl.BlockSpec(memory_space=ANY)] * (len(arrays) - len(specs))
    aliases = {}
    out_shape = jax.ShapeDtypeStruct((rows * fold, LANES), BF16)
    out_specs = pl.BlockSpec(memory_space=HBM)
    if last:
        block = pl.BlockSpec((1, rows, fold * LANES), lambda i, info, *_: (info[0], 0, 0))
        aliases = {2 + len(arrays): 0}
        out_shape = jax.ShapeDtypeStruct(results.shape, BF16)
        arrays, specs, out_specs = arrays + [results], specs + [block], block
    return pl.pallas_call(
        functools.partial(combine_kernel, top is not None, inc is not None, last, rows, fold),
        out_shape=out_shape,
        grid_spec=pltpu.PrefetchScalarGridSpec(
            num_scalar_prefetch=2,
            grid=(1,),
            in_specs=specs,
            out_specs=out_specs,
            scratch_shapes=[
                VM((rows, fold * LANES), BF16),
                VM((rows * fold, LANES), BF16),
                VM((rows * fold, LANES), F32),
                VM((slots * fold, LANES), BF16),
                pltpu.SemaphoreType.DMA((4,)),
            ],
        ),
        input_output_aliases=aliases,
        compiler_params=pltpu.CompilerParams(vmem_limit_bytes=LIMITS["combine"]),
        cost_estimate=estimate(1e6, 4e6),
        name="combine",
    )(info, slot, *arrays)


def keep_kernel(rows, fold, aliased, info_ref, new_ref, *refs):
    old_ref, flat_ref, cur_ref = refs if aliased else (None, *refs)
    cur_ref[...] = new_ref[...].astype(F32)
    if aliased:
        unfold_rows(info_ref, cur_ref, old_ref, flat_ref, rows, fold)
    else:
        flatten_rows(cur_ref, flat_ref.at[0], rows, fold)


def keep_rows(info, new, results, ticks, rows, fold):
    block = pl.BlockSpec((1, rows, fold * LANES), lambda i, info: (info[0], 0, 0))
    more = [] if results is None else [results]
    return pl.pallas_call(
        functools.partial(keep_kernel, rows, fold, results is not None),
        out_shape=jax.ShapeDtypeStruct((ticks, rows, fold * LANES), BF16),
        grid_spec=pltpu.PrefetchScalarGridSpec(
            num_scalar_prefetch=1,
            grid=(1,),
            in_specs=[pl.BlockSpec((rows * fold, LANES), lambda i, info: (0, 0))] + [block] * len(more),
            out_specs=block,
            scratch_shapes=[VM((rows * fold, LANES), F32)],
        ),
        input_output_aliases={2: 0} if more else {},
        compiler_params=PARAMS,
        cost_estimate=estimate(1e6, 1e6),
        name="keep_rows",
    )(info, new, *more)


def gradients_kernel(lead_ref, dg_ref, du_ref, xs_ref, gs_ref, gate_ref, up_ref, down_ref):
    rows_x = xs_ref[...]
    gate_ref[...] = dot(rows_x, dg_ref[...], 0, 0)
    up_ref[...] = dot(rows_x, du_ref[...], 0, 0)
    down_ref[...] = dot(lead_ref[...], gs_ref[...], 1, 0)


def gradients(lead, dg, du, xs, gs):
    depth, width = xs.shape
    hidden = dg.shape[1]
    wide = 256

    def whole(value):
        return pl.BlockSpec(value.shape, lambda i: (0, 0))

    columns = pl.BlockSpec((depth, wide), lambda i: (0, i))
    rows_out = pl.BlockSpec((wide, hidden), lambda i: (i, 0))
    return pl.pallas_call(
        gradients_kernel,
        out_shape=(
            jax.ShapeDtypeStruct((width, hidden), F32),
            jax.ShapeDtypeStruct((width, hidden), F32),
            jax.ShapeDtypeStruct((hidden, width), F32),
        ),
        grid=(width // wide,),
        in_specs=[whole(lead), whole(dg), whole(du), columns, columns],
        out_specs=(rows_out, rows_out, pl.BlockSpec((hidden, wide), lambda i: (0, i))),
        compiler_params=PARAMS,
        cost_estimate=estimate(6 * hidden * width * depth, 18e6),
        name="gradients",
    )(lead, dg, du, xs, gs)


def forward_kernel(aliased, tick, slots, fold, experts, got_hbm, wg_hbm, wu_hbm, *refs):
    refs = list(refs)
    if aliased:
        refs.pop(0)
    xs_hbm, hid_hbm, fac_hbm, got, both_w, scr, xs, hid, fac, sems = refs
    copies = [
        pltpu.make_async_copy(got_hbm.at[:, pl.ds(0, got.shape[1])], got, sems.at[0]),
        pltpu.make_async_copy(wg_hbm, both_w.at[0], sems.at[1]),
        pltpu.make_async_copy(wu_hbm, both_w.at[1], sems.at[2]),
    ]
    for copy in copies:
        copy.start()
    copies[0].wait()
    widen(got, scr, 4)
    flatten_rows(scr, xs, slots, fold)
    puts = [
        pltpu.make_async_copy(xs, xs_hbm.at[pl.ds(tick * slots, slots)], sems.at[3]),
        pltpu.make_async_copy(hid, hid_hbm, sems.at[4]),
        pltpu.make_async_copy(fac, fac_hbm, sems.at[5]),
    ]
    puts[0].start()
    copies[1].wait()
    copies[2].wait()

    if tick == 0:
        gate, up = dot(xs[...], both_w[0], 1, 0), dot(xs[...], both_w[1], 1, 0)
    else:

        def project(which, carry):
            fac[which] = dot(xs[...], both_w[which], 1, 0)
            return carry

        lax.fori_loop(0, 2, project, 0)
        gate, up = fac[0], fac[1]
    logistic = jax.nn.sigmoid(gate)
    soft = gate * logistic
    fac[0] = up * (logistic * (1.0 + gate * (1.0 - logistic)))
    fac[1] = soft
    puts[2].start()
    hid[...] = (soft * up).astype(BF16)
    puts[1].start()
    for put in puts:
        put.wait()


def forward(got, wg, wu, xs_all, tick, ticks, slots, fold, limit):
    experts = got.shape[0]
    width, hidden = wg.shape
    arrays = [got, wg, wu]
    aliases = {}
    if xs_all is not None:
        arrays.append(xs_all)
        aliases = {3: 0}
    hbm_spec = pl.BlockSpec(memory_space=HBM)
    return pl.pallas_call(
        functools.partial(forward_kernel, xs_all is not None, tick, slots, fold, experts),
        out_shape=(
            jax.ShapeDtypeStruct((ticks * slots, width), BF16),
            jax.ShapeDtypeStruct((slots, hidden), BF16),
            jax.ShapeDtypeStruct((2, slots, hidden), F32),
        ),
        in_specs=[pl.BlockSpec(memory_space=ANY)] + [hbm_spec] * (len(arrays) - 1),
        out_specs=(hbm_spec,) * 3,
        scratch_shapes=[
            VM((experts, slots * fold // experts, LANES), BF16),
            VM((2, width, hidden), BF16),
            VM((slots * fold, LANES), F32),
            VM((slots, width), BF16),
            VM((slots, hidden), BF16),
            VM((2, slots, hidden), F32),
            pltpu.SemaphoreType.DMA((6,)),
        ],
        input_output_aliases=aliases,
        compiler_params=pltpu.CompilerParams(vmem_limit_bytes=limit),
        cost_estimate=estimate(4 * slots * width * hidden, 8e6),
        name="forward",
    )(*arrays)


def backward_kernel(
    aliased, count, slots, fold, info_ref, got_hbm, wd_hbm, wg_hbm, wu_hbm, *refs
):
    refs = list(refs)
    fac_hbm = refs[:count]
    del refs[:count]
    if aliased:
        del refs[:3]
    out_hbm, gs_hbm, dg_hbm, du_hbm, got, wd, wg, wu, fac, scr, gs, dg, du, out, sems = refs
    begin = got_hbm.shape[1] - got.shape[1]
    copies = [
        pltpu.make_async_copy(got_hbm.at[:, pl.ds(begin, got.shape[1])], got, sems.at[0]),
        pltpu.make_async_copy(wd_hbm, wd, sems.at[1]),
        pltpu.make_async_copy(wg_hbm, wg, sems.at[2]),
        pltpu.make_async_copy(wu_hbm, wu, sems.at[3]),
    ]
    copies[0].start()
    copies[1].start()
    for which in range(count):

        @pl.when(info_ref[0] == which)
        def _(which=which):
            pltpu.make_async_copy(fac_hbm[which], fac, sems.at[4]).start()

    copies[2].start()
    copies[3].start()
    copies[0].wait()
    widen(got, scr, 4)
    flatten_rows(scr, gs, slots, fold)
    mine = pl.ds(pl.multiple_of(info_ref[0] * slots, slots), slots)
    keeps = [
        pltpu.make_async_copy(gs, gs_hbm.at[mine], sems.at[5]),
        pltpu.make_async_copy(dg, dg_hbm.at[mine], sems.at[6]),
        pltpu.make_async_copy(du, du_hbm.at[mine], sems.at[7]),
    ]
    copies[1].wait()
    grad_hidden = dot(gs[...], wd[...], 1, 1)
    pltpu.make_async_copy(fac_hbm[0], fac, sems.at[4]).wait()
    d_gate = (grad_hidden * fac[0]).astype(BF16)
    d_up = (grad_hidden * fac[1]).astype(BF16)
    dg[...] = d_gate
    du[...] = d_up
    copies[2].wait()
    copies[3].wait()

    @pl.when(info_ref[2] == 1)
    def _():
        for keep in keeps:
            keep.start()

    puts = []
    wide = 4
    for part in range(0, fold, wide):
        cols = slice(part * LANES, (part + wide) * LANES)
        back = dot(d_gate, wg[cols, :], 1, 1) + dot(d_up, wu[cols, :], 1, 1)
        for inner in range(wide):
            scr[pl.ds(part + inner, slots, stride=fold), :] = back[
                :, inner * LANES : (inner + 1) * LANES
            ]
    size = slots * fold // 4
    for chunk in range(4):
        some = pl.ds(chunk * size, size)
        narrow(scr, out, chunk * size, (chunk + 1) * size, 256)
        puts.append(pltpu.make_async_copy(out.at[some], out_hbm.at[some], sems.at[8 + chunk]))
        puts[-1].start()
    for put in puts:
        put.wait()

    @pl.when(info_ref[2] == 1)
    def _():
        for keep in keeps:
            keep.wait()


def backward(info, got, wd, wg, wu, facs, kept, ticks, slots, fold, limit):
    width, hidden = wg.shape
    experts = got.shape[0]
    hbm_spec = pl.BlockSpec(memory_space=HBM)
    arrays = [got, wd, wg, wu, *facs]
    aliases = {}
    if kept is not None:
        aliases = {1 + len(arrays) + i: 1 + i for i in range(3)}
        arrays += list(kept)
    return pl.pallas_call(
        functools.partial(backward_kernel, kept is not None, len(facs), slots, fold),
        out_shape=(
            jax.ShapeDtypeStruct((slots * fold, LANES), BF16),
            jax.ShapeDtypeStruct((ticks * slots, width), BF16),
            jax.ShapeDtypeStruct((ticks * slots, hidden), BF16),
            jax.ShapeDtypeStruct((ticks * slots, hidden), BF16),
        ),
        grid_spec=pltpu.PrefetchScalarGridSpec(
            num_scalar_prefetch=1,
            grid=(1,),
            in_specs=[pl.BlockSpec(memory_space=ANY)] + [hbm_spec] * (len(arrays) - 1),
            out_specs=(hbm_spec,) * 4,
            scratch_shapes=[
                VM((experts, slots * fold // experts, LANES), BF16),
                VM((hidden, width), BF16),
                VM((width, hidden), BF16),
                VM((width, hidden), BF16),
                VM((2, slots, hidden), F32),
                VM((slots * fold, LANES), F32),
                VM((slots, width), BF16),
                VM((slots, hidden), BF16),
                VM((slots, hidden), BF16),
                VM((slots * fold, LANES), BF16),
                pltpu.SemaphoreType.DMA((12,)),
            ],
        ),
        input_output_aliases=aliases,
        compiler_params=pltpu.CompilerParams(vmem_limit_bytes=limit),
        cost_estimate=estimate(6 * slots * width * hidden, 12e6),
        name="backward",
    )(info, *arrays)


def tables(ids, weights, experts, capacity):
    ticks, rows, top = ids.shape
    flat = ids.reshape(ticks, rows * top)
    order = jnp.arange(rows * top, dtype=jnp.int32)
    same = (flat[:, :, None] == flat[:, None, :]) & (order[None, :] < order[:, None])[None]
    target = flat * capacity + same.astype(jnp.int32).sum(axis=2)
    places = jnp.arange(experts * capacity, dtype=jnp.int32)
    chosen = places[None, :, None] == target[:, None, :]
    source = jnp.where(chosen, (order // top)[None, None, :], 0).sum(axis=2)
    scale = jnp.where(chosen, weights.reshape(ticks, 1, rows * top), 0.0).sum(axis=2)
    return target.reshape(-1), source.reshape(-1), scale.reshape(-1)


def split(value):
    high = value.astype(BF16)
    return high, (value - high.astype(F32)).astype(BF16)


def mul(a, b):
    a_high, a_low = split(a)
    b_high, b_low = split(b)
    return dot(a_high, b_high, 1, 0) + (dot(a_high, b_low, 1, 0) + dot(a_low, b_high, 1, 0))


def eye_like(value):
    rows = lax.broadcasted_iota(jnp.int32, value.shape, 0)
    return jnp.where(rows == lax.broadcasted_iota(jnp.int32, value.shape, 1), 1.0, 0.0)


def total_of(value):
    return jnp.sum(jnp.sum(value, axis=1, keepdims=True), axis=0, keepdims=True)


RES, FACTOR, CURRENT = 0, 1, 4


def root_turns(buf_ref, turns):
    def product(step, carry):
        right = jnp.where(step == 0, FACTOR, jnp.where(step == 3, CURRENT, step))
        to = jnp.where(step == 0, RES, step + 1)
        buf_ref[to] = mul(buf_ref[step], buf_ref[right])
        return carry

    def turn(_, carry):
        current = buf_ref[CURRENT]
        buf_ref[FACTOR] = (5.0 * eye_like(current) - current) * 0.25
        return lax.fori_loop(0, 4, product, carry)

    lax.fori_loop(0, turns, turn, 0)


def root_start_kernel(count, turns, *refs):
    state_ref, buf_ref = refs[count:]
    gram = None
    for ref in refs[:count]:
        term = dot(ref[...], ref[...], 0, 0)
        gram = term if gram is None else gram + term
    identity_m = eye_like(gram)
    ratio = gram.shape[0] / (total_of(gram * identity_m) + epsilon)
    curvature = gram * ratio + damping * identity_m
    frobenius = jnp.sqrt(total_of(curvature * curvature))
    buf_ref[CURRENT] = curvature * (1.0 / frobenius)
    buf_ref[RES] = identity_m * lax.rsqrt(jnp.sqrt(frobenius))
    root_turns(buf_ref, turns)
    state_ref[0] = buf_ref[RES]
    state_ref[1] = buf_ref[CURRENT]


def root_more_kernel(turns, state_in, state_ref, buf_ref):
    buf_ref[RES] = state_in[0]
    buf_ref[CURRENT] = state_in[1]
    root_turns(buf_ref, turns)
    state_ref[0] = buf_ref[RES]
    state_ref[1] = buf_ref[CURRENT]


def root_end_kernel(count, state_in, *refs):
    lead_ref, root_ref = refs[count:]
    current = state_in[1]
    root_ref[...] = mul(state_in[0], (5.0 * eye_like(current) - current) * 0.25)
    high, low = split(root_ref[...])
    width = refs[0].shape[0]
    for which, ref in enumerate(refs[:count]):
        lead = dot(high, ref[...], 1, 1) + dot(low, ref[...], 1, 1)
        lead_ref[:, which * width : (which + 1) * width] = lead.astype(BF16)


def root_call(kernel, name, out_shape, flops, scratch, *arrays):
    whole = pl.BlockSpec(memory_space=pltpu.VMEM)
    return pl.pallas_call(
        kernel,
        out_shape=out_shape,
        in_specs=[whole] * len(arrays),
        out_specs=whole,
        scratch_shapes=[scratch],
        compiler_params=pltpu.CompilerParams(vmem_limit_bytes=LIMITS["root"]),
        cost_estimate=estimate(flops, 4e6),
        name=name,
    )(*arrays)


def shards(section_inputs, cotangent, expert_ids, route_weights, w_gate, w_up, w_down):
    section = lax.axis_index("section")
    sections = lax.axis_size("section")
    experts = lax.axis_size("expert")
    _, ticks, rows, width = section_inputs.shape
    fold = width // LANES
    capacity = max(2, 3 * rows // experts)
    slots = experts * capacity
    wg, wu, wd = w_gate[0, 0], w_up[0, 0], w_down[0, 0]
    hidden = wg.shape[1]

    slot, src, scale = tables(expert_ids[0], route_weights[0], experts, capacity)
    x_rows = section_inputs[0]

    def exchange(value):
        return lax.all_to_all(
            value.reshape(experts, -1, LANES), "expert", split_axis=0, concat_axis=0, tiled=True
        )

    def pack(info, tops, inc, plain):
        return dispatch(info, src, scale, tops, inc, plain, rows, slots, fold, capacity)

    steps = sections - 1 + ticks
    start = sections - 1 - section
    is_top = (section == sections - 1).astype(jnp.int32)
    infos = []
    for step in range(steps):
        offset = step - start
        active = ((offset >= 0) & (offset < ticks)).astype(jnp.int32)
        infos.append(jnp.stack([jnp.clip(offset, 0, ticks - 1), is_top, active]).astype(jnp.int32))

    xs_all, hiddens, facs = None, [], []
    pair = jax.ShapeDtypeStruct((2, hidden, hidden), F32)
    work = VM((5, hidden, hidden), F32)
    product = 6 * hidden**3

    def root_part(part, beside):
        if part == 0:
            kernel = functools.partial(root_start_kernel, ticks, 2)
            value = root_call(kernel, "root_start", pair, 8 * product, work, *hiddens)
        elif part == 1:
            kernel = functools.partial(root_more_kernel, NS_ITERS - 3)
            value = root_call(kernel, "root_more", pair, 8 * product, work, state)
        else:
            shape = jax.ShapeDtypeStruct((hidden, ticks * slots), BF16)
            kernel = functools.partial(root_end_kernel, ticks)
            one = VM((hidden, hidden), F32)
            value = root_call(kernel, "root_end", shape, 3 * product, one, state, *hiddens)
        return lax.optimization_barrier((beside, value))

    both = exchange(first_dispatch(src, scale, x_rows, cotangent, rows, slots, fold, capacity))
    got_x = {0: both}
    kept, results, inc = None, None, None
    for step in range(steps):
        info = infos[step]
        tops = cotangent if step < ticks else None
        got = exchange(pack(info, tops, inc, False)) if step else both
        limit = LIMITS["backward"] if step else LIMITS["first"]
        if step < ticks:
            xs_all, hid, fac = forward(got_x[step], wg, wu, xs_all, step, ticks, slots, fold, LIMITS["forward"] if step else limit)
            hiddens.append(hid)
            facs.append(fac)
        sent, *kept = backward(info, got, wd, wg, wu, facs, kept, ticks, slots, fold, limit)
        came = exchange(sent).reshape(slots * fold, LANES)
        part = step - (ticks - 1)
        if part in (0, 1):
            came, state = root_part(part, came)
        if part == 2:
            came, lead = root_part(part, came)
        if step < steps - 1:
            new = combine(info, slot, tops, inc, came, rows, slots, fold)
            if step + 1 < ticks:
                more = pack(jnp.array([step + 1, 1, 1], jnp.int32), x_rows, None, True)
                new, more = lax.optimization_barrier((new, more))
            results = keep_rows(info, new, results, ticks, rows, fold)
            inc = lax.ppermute(new, "section", [(s, s - 1) for s in range(1, sections)])
            inc, results = lax.optimization_barrier((inc, results))
        else:
            results = combine(info, slot, tops, inc, came, rows, slots, fold, results)
        if step + 1 < ticks:
            got_x[step + 1] = exchange(more)

    gs, dg, du = kept
    grad_gate, grad_up, precond = gradients(lead, dg, du, xs_all, gs)
    return (results[None], grad_gate[None, None], grad_up[None, None], precond[None, None])


def solution(mesh):
    return jax.shard_map(
        shards,
        mesh=mesh,
        in_specs=(
            P("section", None, "expert", None),
            P(None, "expert", None),
            P("section", None, "expert", None),
            P("section", None, "expert", None),
            P("section", "expert", None, None),
            P("section", "expert", None, None),
            P("section", "expert", None, None),
        ),
        out_specs=(
            P("section", None, "expert", None),
            P("section", "expert", None, None),
            P("section", "expert", None, None),
            P("section", "expert", None, None),
        ),
        check_vma=False,
    )
```

```python
import functools

import jax
import jax.numpy as jnp
from jax import lax
from jax.experimental import pallas as pl
from jax.experimental.pallas import tpu as pltpu
from jax.sharding import PartitionSpec as P

NS_ITERS = 5

damping = 0.1
epsilon = 1e-06

LANES = 128
F32 = jnp.float32
BF16 = jnp.bfloat16
VM = pltpu.VMEM
SM = pltpu.SMEM
PARAMS = pltpu.CompilerParams(vmem_limit_bytes=60 << 20)
LIMITS = {"root": 62000000, "dispatch": 55000000, "backward": 53500000, "combine": 54000000, "first": 53500000, "forward": 62000000}


def estimate(flops, moved):
    return pl.CostEstimate(flops=int(flops), bytes_accessed=int(moved), transcendentals=0)


def dot(a, b, ad, bd):
    return lax.dot_general(a, b, (((ad,), (bd,)), ((), ())), preferred_element_type=F32)


HBM = pltpu.HBM
ANY = pl.ANY


def lanes_of(part):
    return pl.ds(pl.multiple_of(part * LANES, LANES), LANES)


def fold_rows(flat_ref, cur_ref, rows, fold):
    def some(part, carry):
        cur_ref[pl.ds(part, rows, stride=fold), :] = flat_ref[:, lanes_of(part)].astype(F32)
        return carry

    lax.fori_loop(0, fold, some, 0)


def flatten_rows(cur_ref, flat_ref, rows, fold):
    def some(part, carry):
        flat_ref[:, lanes_of(part)] = cur_ref[pl.ds(part, rows, stride=fold), :].astype(BF16)
        return carry

    lax.fori_loop(0, fold, some, 0)


def widen(got_ref, cur_ref, group):
    count, depth, _ = got_ref.shape

    def some(step, carry):
        part = got_ref[pl.ds(step * group, group)].astype(F32)
        here = pl.ds(pl.multiple_of(step * group * depth, group * depth), group * depth)
        cur_ref[here, :] = part.reshape(group * depth, LANES)
        return carry

    lax.fori_loop(0, count // group, some, 0)


def narrow(cur_ref, out_ref, begin, end, size):
    def some(step, carry):
        here = pl.ds(pl.multiple_of(step * size, size), size)
        out_ref[here, :] = cur_ref[here, :].astype(BF16)
        return carry

    lax.fori_loop(begin // size, end // size, some, 0)


def load_current(info_ref, top_ref, inc_ref, flat_ref, buf_ref, cur_ref, sem, rows, fold):
    def from_top():
        copy = pltpu.make_async_copy(top_ref.at[info_ref[0]], flat_ref, sem)
        copy.start()
        copy.wait()
        fold_rows(flat_ref, cur_ref, rows, fold)

    def from_above():
        copy = pltpu.make_async_copy(inc_ref, buf_ref, sem)
        copy.start()
        copy.wait()
        cur_ref[...] = buf_ref[...].astype(F32)

    if inc_ref is None:
        from_top()
    elif top_ref is None:
        from_above()
    else:
        pl.when(info_ref[1] == 1)(from_top)
        pl.when(info_ref[1] == 0)(from_above)


def place_rows(
    src_ref, scale_ref, plain, base, first, count, fold, group, stride, offset, cur_ref, out_ref
):
    def some(step, carry):
        for part in range(group):
            place = step * group + part
            row = src_ref[base + place]
            factor = scale_ref[base + place]
            if plain:
                factor = jnp.where(factor > 0.0, 1.0, 0.0)
            tile = cur_ref[pl.ds(pl.multiple_of(row * fold, fold), fold), :]
            out_ref[pl.ds(pl.multiple_of((step * stride + offset + part) * fold, fold), fold), :] = (
                tile * factor
            ).astype(BF16)
        return carry

    lax.fori_loop(first // group, (first + count) // group, some, 0)


CHUNKS = 1
FIRST_CHUNKS = 2


def dispatch_kernel(
    has_top, has_inc, plain, rows, slots, fold, group, info_ref, src_ref, scale_ref, *refs
):
    refs = list(refs)
    top_ref = refs.pop(0) if has_top else None
    inc_ref = refs.pop(0) if has_inc else None
    out_ref, flat_ref, buf_ref, cur_ref, put_ref, sems = refs
    load_current(info_ref, top_ref, inc_ref, flat_ref, buf_ref, cur_ref, sems.at[0], rows, fold)
    base = info_ref[0] * slots
    count = slots // CHUNKS
    copies = []
    for chunk in range(CHUNKS):
        place_rows(
            src_ref, scale_ref, plain, base, chunk * count, count, fold, group, group, 0,
            cur_ref, put_ref,
        )
        part = pl.ds(chunk * count * fold, count * fold)
        copies.append(
            pltpu.make_async_copy(put_ref.at[part], out_ref.at[part], sems.at[1 + chunk])
        )
        copies[-1].start()
    for copy in copies:
        copy.wait()


def dispatch(info, src, scale, top, inc, plain, rows, slots, fold, group):
    arrays = [value for value in (top, inc) if value is not None]
    return pl.pallas_call(
        functools.partial(
            dispatch_kernel, top is not None, inc is not None, plain, rows, slots, fold, group
        ),
        out_shape=jax.ShapeDtypeStruct((slots * fold, LANES), BF16),
        grid_spec=pltpu.PrefetchScalarGridSpec(
            num_scalar_prefetch=2,
            grid=(1,),
            in_specs=[pl.BlockSpec(memory_space=SM)]
            + [pl.BlockSpec(memory_space=HBM)] * (top is not None)
            + [pl.BlockSpec(memory_space=ANY)] * (inc is not None),
            out_specs=pl.BlockSpec(memory_space=HBM),
            scratch_shapes=[
                VM((rows, fold * LANES), BF16),
                VM((rows * fold, LANES), BF16),
                VM((rows * fold, LANES), F32),
                VM((slots * fold, LANES), BF16),
                pltpu.SemaphoreType.DMA((1 + CHUNKS,)),
            ],
        ),
        compiler_params=pltpu.CompilerParams(vmem_limit_bytes=LIMITS["dispatch"]),
        cost_estimate=estimate(1e6, 4e6),
        name="dispatch",
    )(info, src, scale, *arrays)


def first_kernel(rows, slots, fold, group, src_ref, scale_ref, x_ref, top_ref, out_ref, *rest):
    buf_x, buf_g, cur_x, cur_g, put_ref, sems = rest
    copies = [
        pltpu.make_async_copy(x_ref.at[0], buf_x, sems.at[0]),
        pltpu.make_async_copy(top_ref.at[0], buf_g, sems.at[1]),
    ]
    for copy in copies:
        copy.start()
    copies[0].wait()
    fold_rows(buf_x, cur_x, rows, fold)
    copies[1].wait()
    fold_rows(buf_g, cur_g, rows, fold)
    count = slots // FIRST_CHUNKS
    copies = []
    for chunk in range(FIRST_CHUNKS):
        for offset, plain, cur in ((0, True, cur_x), (group, False, cur_g)):
            place_rows(
                src_ref, scale_ref, plain, 0, chunk * count, count, fold, group, 2 * group, offset,
                cur, put_ref,
            )
        part = pl.ds(chunk * count * fold * 2, count * fold * 2)
        copies.append(
            pltpu.make_async_copy(put_ref.at[part], out_ref.at[part], sems.at[2 + chunk])
        )
        copies[-1].start()
    for copy in copies:
        copy.wait()


def first_dispatch(src, scale, x, top, rows, slots, fold, group):
    return pl.pallas_call(
        functools.partial(first_kernel, rows, slots, fold, group),
        out_shape=jax.ShapeDtypeStruct((2 * slots * fold, LANES), BF16),
        in_specs=[pl.BlockSpec(memory_space=SM)] * 2 + [pl.BlockSpec(memory_space=HBM)] * 2,
        out_specs=pl.BlockSpec(memory_space=HBM),
        scratch_shapes=[VM((rows, fold * LANES), BF16)] * 2
        + [VM((rows * fold, LANES), F32)] * 2
        + [VM((2 * slots * fold, LANES), BF16), pltpu.SemaphoreType.DMA((2 + FIRST_CHUNKS,))],
        compiler_params=PARAMS,
        cost_estimate=estimate(1e6, 4e6),
        name="first_dispatch",
    )(src, scale, x, top)


def combine_kernel(has_top, has_inc, last, rows, fold, info_ref, slot_ref, *refs):
    refs = list(refs)
    top_ref = refs.pop(0) if has_top else None
    inc_ref = refs.pop(0) if has_inc else None
    came_hbm = refs.pop(0)
    if last:
        old_ref, flat_ref, top_buf, buf_ref, cur_ref, came_ref, sems = refs
    else:
        new_ref, top_buf, buf_ref, cur_ref, came_ref, sems = refs
    came_copy = pltpu.make_async_copy(came_hbm, came_ref, sems.at[1])
    came_copy.start()
    load_current(info_ref, top_ref, inc_ref, top_buf, buf_ref, cur_ref, sems.at[0], rows, fold)
    came_copy.wait()
    base = info_ref[0] * rows * 2

    def some(step, carry):
        for part in range(4):
            row = step * 4 + part
            first = slot_ref[base + 2 * row]
            second = slot_ref[base + 2 * row + 1]
            here = pl.ds(pl.multiple_of(row * fold, fold), fold)
            one = came_ref[pl.ds(pl.multiple_of(first * fold, fold), fold), :].astype(F32)
            two = came_ref[pl.ds(pl.multiple_of(second * fold, fold), fold), :].astype(F32)
            total = cur_ref[here, :] + (one + two)
            if last:
                cur_ref[here, :] = total
            else:
                buf_ref[here, :] = total.astype(BF16)
        return carry

    if not last:
        half = rows // 2
        copies = []
        for chunk in range(2):
            lax.fori_loop(chunk * half // 4, (chunk + 1) * half // 4, some, 0)
            part = pl.ds(chunk * half * fold, half * fold)
            copies.append(
                pltpu.make_async_copy(buf_ref.at[part], new_ref.at[part], sems.at[2 + chunk])
            )
            copies[-1].start()
        for copy in copies:
            copy.wait()
    else:
        lax.fori_loop(0, rows // 4, some, 0)
        unfold_rows(info_ref, cur_ref, old_ref, flat_ref, rows, fold)


def unfold_rows(info_ref, cur_ref, old_ref, flat_ref, rows, fold):
    @pl.when(info_ref[2] == 1)
    def _():
        flatten_rows(cur_ref, flat_ref.at[0], rows, fold)

    @pl.when(info_ref[2] == 0)
    def _():
        flat_ref[...] = old_ref[...]


def combine(info, slot, top, inc, came, rows, slots, fold, results=None):
    last = results is not None
    arrays = [value for value in (top, inc, came) if value is not None]
    specs = [pl.BlockSpec(memory_space=HBM)] * (top is not None)
    specs += [pl.BlockSpec(memory_space=ANY)] * (len(arrays) - len(specs))
    aliases = {}
    out_shape = jax.ShapeDtypeStruct((rows * fold, LANES), BF16)
    out_specs = pl.BlockSpec(memory_space=HBM)
    if last:
        block = pl.BlockSpec((1, rows, fold * LANES), lambda i, info, *_: (info[0], 0, 0))
        aliases = {2 + len(arrays): 0}
        out_shape = jax.ShapeDtypeStruct(results.shape, BF16)
        arrays, specs, out_specs = arrays + [results], specs + [block], block
    return pl.pallas_call(
        functools.partial(combine_kernel, top is not None, inc is not None, last, rows, fold),
        out_shape=out_shape,
        grid_spec=pltpu.PrefetchScalarGridSpec(
            num_scalar_prefetch=2,
            grid=(1,),
            in_specs=specs,
            out_specs=out_specs,
            scratch_shapes=[
                VM((rows, fold * LANES), BF16),
                VM((rows * fold, LANES), BF16),
                VM((rows * fold, LANES), F32),
                VM((slots * fold, LANES), BF16),
                pltpu.SemaphoreType.DMA((4,)),
            ],
        ),
        input_output_aliases=aliases,
        compiler_params=pltpu.CompilerParams(vmem_limit_bytes=LIMITS["combine"]),
        cost_estimate=estimate(1e6, 4e6),
        name="combine",
    )(info, slot, *arrays)


def keep_kernel(rows, fold, aliased, info_ref, new_ref, *refs):
    old_ref, flat_ref, cur_ref = refs if aliased else (None, *refs)
    cur_ref[...] = new_ref[...].astype(F32)
    if aliased:
        unfold_rows(info_ref, cur_ref, old_ref, flat_ref, rows, fold)
    else:
        flatten_rows(cur_ref, flat_ref.at[0], rows, fold)


def keep_rows(info, new, results, ticks, rows, fold):
    block = pl.BlockSpec((1, rows, fold * LANES), lambda i, info: (info[0], 0, 0))
    more = [] if results is None else [results]
    return pl.pallas_call(
        functools.partial(keep_kernel, rows, fold, results is not None),
        out_shape=jax.ShapeDtypeStruct((ticks, rows, fold * LANES), BF16),
        grid_spec=pltpu.PrefetchScalarGridSpec(
            num_scalar_prefetch=1,
            grid=(1,),
            in_specs=[pl.BlockSpec((rows * fold, LANES), lambda i, info: (0, 0))] + [block] * len(more),
            out_specs=block,
            scratch_shapes=[VM((rows * fold, LANES), F32)],
        ),
        input_output_aliases={2: 0} if more else {},
        compiler_params=PARAMS,
        cost_estimate=estimate(1e6, 1e6),
        name="keep_rows",
    )(info, new, *more)


def gradients_kernel(lead_ref, dg_ref, du_ref, xs_ref, gs_ref, gate_ref, up_ref, down_ref):
    rows_x = xs_ref[...]
    gate_ref[...] = dot(rows_x, dg_ref[...], 0, 0)
    up_ref[...] = dot(rows_x, du_ref[...], 0, 0)
    down_ref[...] = dot(lead_ref[...], gs_ref[...], 1, 0)


def gradients(lead, dg, du, xs, gs):
    depth, width = xs.shape
    hidden = dg.shape[1]
    wide = 256

    def whole(value):
        return pl.BlockSpec(value.shape, lambda i: (0, 0))

    columns = pl.BlockSpec((depth, wide), lambda i: (0, i))
    rows_out = pl.BlockSpec((wide, hidden), lambda i: (i, 0))
    return pl.pallas_call(
        gradients_kernel,
        out_shape=(
            jax.ShapeDtypeStruct((width, hidden), F32),
            jax.ShapeDtypeStruct((width, hidden), F32),
            jax.ShapeDtypeStruct((hidden, width), F32),
        ),
        grid=(width // wide,),
        in_specs=[whole(lead), whole(dg), whole(du), columns, columns],
        out_specs=(rows_out, rows_out, pl.BlockSpec((hidden, wide), lambda i: (0, i))),
        compiler_params=PARAMS,
        cost_estimate=estimate(6 * hidden * width * depth, 18e6),
        name="gradients",
    )(lead, dg, du, xs, gs)


def forward_kernel(aliased, tick, slots, fold, experts, got_hbm, wg_hbm, wu_hbm, *refs):
    refs = list(refs)
    if aliased:
        refs.pop(0)
    xs_hbm, hid_hbm, fac_hbm, got, both_w, scr, xs, hid, fac, sems = refs
    copies = [
        pltpu.make_async_copy(got_hbm.at[:, pl.ds(0, got.shape[1])], got, sems.at[0]),
        pltpu.make_async_copy(wg_hbm, both_w.at[0], sems.at[1]),
        pltpu.make_async_copy(wu_hbm, both_w.at[1], sems.at[2]),
    ]
    for copy in copies:
        copy.start()
    copies[0].wait()
    widen(got, scr, 4)
    flatten_rows(scr, xs, slots, fold)
    puts = [
        pltpu.make_async_copy(xs, xs_hbm.at[pl.ds(tick * slots, slots)], sems.at[3]),
        pltpu.make_async_copy(hid, hid_hbm, sems.at[4]),
        pltpu.make_async_copy(fac, fac_hbm, sems.at[5]),
    ]
    puts[0].start()
    copies[1].wait()
    copies[2].wait()

    if tick == 0:
        gate, up = dot(xs[...], both_w[0], 1, 0), dot(xs[...], both_w[1], 1, 0)
    else:

        def project(which, carry):
            fac[which] = dot(xs[...], both_w[which], 1, 0)
            return carry

        lax.fori_loop(0, 2, project, 0)
        gate, up = fac[0], fac[1]
    logistic = jax.nn.sigmoid(gate)
    soft = gate * logistic
    fac[0] = up * (logistic * (1.0 + gate * (1.0 - logistic)))
    fac[1] = soft
    puts[2].start()
    hid[...] = (soft * up).astype(BF16)
    puts[1].start()
    for put in puts:
        put.wait()


def forward(got, wg, wu, xs_all, tick, ticks, slots, fold, limit):
    experts = got.shape[0]
    width, hidden = wg.shape
    arrays = [got, wg, wu]
    aliases = {}
    if xs_all is not None:
        arrays.append(xs_all)
        aliases = {3: 0}
    hbm_spec = pl.BlockSpec(memory_space=HBM)
    return pl.pallas_call(
        functools.partial(forward_kernel, xs_all is not None, tick, slots, fold, experts),
        out_shape=(
            jax.ShapeDtypeStruct((ticks * slots, width), BF16),
            jax.ShapeDtypeStruct((slots, hidden), BF16),
            jax.ShapeDtypeStruct((2, slots, hidden), F32),
        ),
        in_specs=[pl.BlockSpec(memory_space=ANY)] + [hbm_spec] * (len(arrays) - 1),
        out_specs=(hbm_spec,) * 3,
        scratch_shapes=[
            VM((experts, slots * fold // experts, LANES), BF16),
            VM((2, width, hidden), BF16),
            VM((slots * fold, LANES), F32),
            VM((slots, width), BF16),
            VM((slots, hidden), BF16),
            VM((2, slots, hidden), F32),
            pltpu.SemaphoreType.DMA((6,)),
        ],
        input_output_aliases=aliases,
        compiler_params=pltpu.CompilerParams(vmem_limit_bytes=limit),
        cost_estimate=estimate(4 * slots * width * hidden, 8e6),
        name="forward",
    )(*arrays)


def backward_kernel(
    aliased, count, slots, fold, info_ref, got_hbm, wd_hbm, wg_hbm, wu_hbm, *refs
):
    refs = list(refs)
    fac_hbm = refs[:count]
    del refs[:count]
    if aliased:
        del refs[:3]
    out_hbm, gs_hbm, dg_hbm, du_hbm, got, wd, wg, wu, fac, scr, gs, dg, du, out, sems = refs
    begin = got_hbm.shape[1] - got.shape[1]
    copies = [
        pltpu.make_async_copy(got_hbm.at[:, pl.ds(begin, got.shape[1])], got, sems.at[0]),
        pltpu.make_async_copy(wd_hbm, wd, sems.at[1]),
        pltpu.make_async_copy(wg_hbm, wg, sems.at[2]),
        pltpu.make_async_copy(wu_hbm, wu, sems.at[3]),
    ]
    copies[0].start()
    copies[1].start()
    for which in range(count):

        @pl.when(info_ref[0] == which)
        def _(which=which):
            pltpu.make_async_copy(fac_hbm[which], fac, sems.at[4]).start()

    copies[2].start()
    copies[3].start()
    copies[0].wait()
    widen(got, scr, 4)
    flatten_rows(scr, gs, slots, fold)
    mine = pl.ds(pl.multiple_of(info_ref[0] * slots, slots), slots)
    keeps = [
        pltpu.make_async_copy(gs, gs_hbm.at[mine], sems.at[5]),
        pltpu.make_async_copy(dg, dg_hbm.at[mine], sems.at[6]),
        pltpu.make_async_copy(du, du_hbm.at[mine], sems.at[7]),
    ]
    copies[1].wait()
    grad_hidden = dot(gs[...], wd[...], 1, 1)
    pltpu.make_async_copy(fac_hbm[0], fac, sems.at[4]).wait()
    d_gate = (grad_hidden * fac[0]).astype(BF16)
    d_up = (grad_hidden * fac[1]).astype(BF16)
    dg[...] = d_gate
    du[...] = d_up
    copies[2].wait()
    copies[3].wait()

    @pl.when(info_ref[2] == 1)
    def _():
        for keep in keeps:
            keep.start()

    puts = []
    wide = 4
    for part in range(0, fold, wide):
        cols = slice(part * LANES, (part + wide) * LANES)
        back = dot(d_gate, wg[cols, :], 1, 1) + dot(d_up, wu[cols, :], 1, 1)
        for inner in range(wide):
            scr[pl.ds(part + inner, slots, stride=fold), :] = back[
                :, inner * LANES : (inner + 1) * LANES
            ]
    size = slots * fold // 4
    for chunk in range(4):
        some = pl.ds(chunk * size, size)
        narrow(scr, out, chunk * size, (chunk + 1) * size, 256)
        puts.append(pltpu.make_async_copy(out.at[some], out_hbm.at[some], sems.at[8 + chunk]))
        puts[-1].start()
    for put in puts:
        put.wait()

    @pl.when(info_ref[2] == 1)
    def _():
        for keep in keeps:
            keep.wait()


def backward(info, got, wd, wg, wu, facs, kept, ticks, slots, fold, limit):
    width, hidden = wg.shape
    experts = got.shape[0]
    hbm_spec = pl.BlockSpec(memory_space=HBM)
    arrays = [got, wd, wg, wu, *facs]
    aliases = {}
    if kept is not None:
        aliases = {1 + len(arrays) + i: 1 + i for i in range(3)}
        arrays += list(kept)
    return pl.pallas_call(
        functools.partial(backward_kernel, kept is not None, len(facs), slots, fold),
        out_shape=(
            jax.ShapeDtypeStruct((slots * fold, LANES), BF16),
            jax.ShapeDtypeStruct((ticks * slots, width), BF16),
            jax.ShapeDtypeStruct((ticks * slots, hidden), BF16),
            jax.ShapeDtypeStruct((ticks * slots, hidden), BF16),
        ),
        grid_spec=pltpu.PrefetchScalarGridSpec(
            num_scalar_prefetch=1,
            grid=(1,),
            in_specs=[pl.BlockSpec(memory_space=ANY)] + [hbm_spec] * (len(arrays) - 1),
            out_specs=(hbm_spec,) * 4,
            scratch_shapes=[
                VM((experts, slots * fold // experts, LANES), BF16),
                VM((hidden, width), BF16),
                VM((width, hidden), BF16),
                VM((width, hidden), BF16),
                VM((2, slots, hidden), F32),
                VM((slots * fold, LANES), F32),
                VM((slots, width), BF16),
                VM((slots, hidden), BF16),
                VM((slots, hidden), BF16),
                VM((slots * fold, LANES), BF16),
                pltpu.SemaphoreType.DMA((12,)),
            ],
        ),
        input_output_aliases=aliases,
        compiler_params=pltpu.CompilerParams(vmem_limit_bytes=limit),
        cost_estimate=estimate(6 * slots * width * hidden, 12e6),
        name="backward",
    )(info, *arrays)


def tables(ids, weights, experts, capacity):
    ticks, rows, top = ids.shape
    flat = ids.reshape(ticks, rows * top)
    order = jnp.arange(rows * top, dtype=jnp.int32)
    same = (flat[:, :, None] == flat[:, None, :]) & (order[None, :] < order[:, None])[None]
    target = flat * capacity + same.astype(jnp.int32).sum(axis=2)
    places = jnp.arange(experts * capacity, dtype=jnp.int32)
    chosen = places[None, :, None] == target[:, None, :]
    source = jnp.where(chosen, (order // top)[None, None, :], 0).sum(axis=2)
    scale = jnp.where(chosen, weights.reshape(ticks, 1, rows * top), 0.0).sum(axis=2)
    return target.reshape(-1), source.reshape(-1), scale.reshape(-1)


def split(value):
    high = value.astype(BF16)
    return high, (value - high.astype(F32)).astype(BF16)


def mul(a, b):
    a_high, a_low = split(a)
    b_high, b_low = split(b)
    return dot(a_high, b_high, 1, 0) + (dot(a_high, b_low, 1, 0) + dot(a_low, b_high, 1, 0))


def eye_like(value):
    rows = lax.broadcasted_iota(jnp.int32, value.shape, 0)
    return jnp.where(rows == lax.broadcasted_iota(jnp.int32, value.shape, 1), 1.0, 0.0)


def total_of(value):
    return jnp.sum(jnp.sum(value, axis=1, keepdims=True), axis=0, keepdims=True)


RES, FACTOR, CURRENT = 0, 1, 4


def root_turns(buf_ref, turns):
    def product(step, carry):
        right = jnp.where(step == 0, FACTOR, jnp.where(step == 3, CURRENT, step))
        to = jnp.where(step == 0, RES, step + 1)
        buf_ref[to] = mul(buf_ref[step], buf_ref[right])
        return carry

    def turn(_, carry):
        current = buf_ref[CURRENT]
        buf_ref[FACTOR] = (5.0 * eye_like(current) - current) * 0.25
        return lax.fori_loop(0, 4, product, carry)

    lax.fori_loop(0, turns, turn, 0)


def root_start_kernel(count, turns, *refs):
    state_ref, buf_ref = refs[count:]
    gram = None
    for ref in refs[:count]:
        term = dot(ref[...], ref[...], 0, 0)
        gram = term if gram is None else gram + term
    identity_m = eye_like(gram)
    ratio = gram.shape[0] / (total_of(gram * identity_m) + epsilon)
    curvature = gram * ratio + damping * identity_m
    frobenius = jnp.sqrt(total_of(curvature * curvature))
    buf_ref[CURRENT] = curvature * (1.0 / frobenius)
    buf_ref[RES] = identity_m * lax.rsqrt(jnp.sqrt(frobenius))
    root_turns(buf_ref, turns)
    state_ref[0] = buf_ref[RES]
    state_ref[1] = buf_ref[CURRENT]


def root_more_kernel(turns, state_in, state_ref, buf_ref):
    buf_ref[RES] = state_in[0]
    buf_ref[CURRENT] = state_in[1]
    root_turns(buf_ref, turns)
    state_ref[0] = buf_ref[RES]
    state_ref[1] = buf_ref[CURRENT]


def root_end_kernel(count, state_in, *refs):
    lead_ref, root_ref = refs[count:]
    current = state_in[1]
    root_ref[...] = mul(state_in[0], (5.0 * eye_like(current) - current) * 0.25)
    high, low = split(root_ref[...])
    width = refs[0].shape[0]
    for which, ref in enumerate(refs[:count]):
        lead = dot(high, ref[...], 1, 1) + dot(low, ref[...], 1, 1)
        lead_ref[:, which * width : (which + 1) * width] = lead.astype(BF16)


def root_call(kernel, name, out_shape, flops, scratch, *arrays):
    whole = pl.BlockSpec(memory_space=pltpu.VMEM)
    return pl.pallas_call(
        kernel,
        out_shape=out_shape,
        in_specs=[whole] * len(arrays),
        out_specs=whole,
        scratch_shapes=[scratch],
        compiler_params=pltpu.CompilerParams(vmem_limit_bytes=LIMITS["root"]),
        cost_estimate=estimate(flops, 4e6),
        name=name,
    )(*arrays)


def shards(section_inputs, cotangent, expert_ids, route_weights, w_gate, w_up, w_down):
    section = lax.axis_index("section")
    sections = lax.axis_size("section")
    experts = lax.axis_size("expert")
    _, ticks, rows, width = section_inputs.shape
    fold = width // LANES
    capacity = max(2, 3 * rows // experts)
    slots = experts * capacity
    wg, wu, wd = w_gate[0, 0], w_up[0, 0], w_down[0, 0]
    hidden = wg.shape[1]

    slot, src, scale = tables(expert_ids[0], route_weights[0], experts, capacity)
    x_rows = section_inputs[0]

    def exchange(value):
        return lax.all_to_all(
            value.reshape(experts, -1, LANES), "expert", split_axis=0, concat_axis=0, tiled=True
        )

    def pack(info, tops, inc, plain):
        return dispatch(info, src, scale, tops, inc, plain, rows, slots, fold, capacity)

    steps = sections - 1 + ticks
    start = sections - 1 - section
    is_top = (section == sections - 1).astype(jnp.int32)
    infos = []
    for step in range(steps):
        offset = step - start
        active = ((offset >= 0) & (offset < ticks)).astype(jnp.int32)
        infos.append(jnp.stack([jnp.clip(offset, 0, ticks - 1), is_top, active]).astype(jnp.int32))

    xs_all, hiddens, facs = None, [], []
    pair = jax.ShapeDtypeStruct((2, hidden, hidden), F32)
    work = VM((5, hidden, hidden), F32)
    product = 6 * hidden**3

    def root_part(part, beside):
        if part == 0:
            kernel = functools.partial(root_start_kernel, ticks, 2)
            value = root_call(kernel, "root_start", pair, 8 * product, work, *hiddens)
        elif part == 1:
            kernel = functools.partial(root_more_kernel, NS_ITERS - 3)
            value = root_call(kernel, "root_more", pair, 8 * product, work, state)
        else:
            shape = jax.ShapeDtypeStruct((hidden, ticks * slots), BF16)
            kernel = functools.partial(root_end_kernel, ticks)
            one = VM((hidden, hidden), F32)
            value = root_call(kernel, "root_end", shape, 3 * product, one, state, *hiddens)
        return lax.optimization_barrier((beside, value))

    both = exchange(first_dispatch(src, scale, x_rows, cotangent, rows, slots, fold, capacity))
    got_x = {0: both}
    kept, results, inc = None, None, None
    for step in range(steps):
        info = infos[step]
        tops = cotangent if step < ticks else None
        got = exchange(pack(info, tops, inc, False)) if step else both
        limit = LIMITS["backward"] if step else LIMITS["first"]
        if step < ticks:
            xs_all, hid, fac = forward(got_x[step], wg, wu, xs_all, step, ticks, slots, fold, LIMITS["forward"] if step else limit)
            hiddens.append(hid)
            facs.append(fac)
        sent, *kept = backward(info, got, wd, wg, wu, facs, kept, ticks, slots, fold, limit)
        came = exchange(sent).reshape(slots * fold, LANES)
        part = step - (ticks - 1)
        if part in (0, 1):
            came, state = root_part(part, came)
        if part == 2:
            came, lead = root_part(part, came)
        if step < steps - 1:
            new = combine(info, slot, tops, inc, came, rows, slots, fold)
            if step + 1 < ticks:
                more = pack(jnp.array([step + 1, 1, 1], jnp.int32), x_rows, None, True)
                new, more = lax.optimization_barrier((new, more))
            results = keep_rows(info, new, results, ticks, rows, fold)
            inc = lax.ppermute(new, "section", [(s, s - 1) for s in range(1, sections)])
            inc, results = lax.optimization_barrier((inc, results))
        else:
            results = combine(info, slot, tops, inc, came, rows, slots, fold, results)
        if step + 1 < ticks:
            got_x[step + 1] = exchange(more)

    gs, dg, du = kept
    grad_gate, grad_up, precond = gradients(lead, dg, du, xs_all, gs)
    return (results[None], grad_gate[None, None], grad_up[None, None], precond[None, None])


def solution(mesh):
    return jax.shard_map(
        shards,
        mesh=mesh,
        in_specs=(
            P("section", None, "expert", None),
            P(None, "expert", None),
            P("section", None, "expert", None),
            P("section", None, "expert", None),
            P("section", "expert", None, None),
            P("section", "expert", None, None),
            P("section", "expert", None, None),
        ),
        out_specs=(
            P("section", None, "expert", None),
            P("section", "expert", None, None),
            P("section", "expert", None, None),
            P("section", "expert", None, None),
        ),
        check_vma=False,
    )
```
